256 devices in a mesh: group: 4 (over x), member: 64 (over y, z, core).
Axes of the slice: x: 4, y: 4, z: 8, core: 2. Of those that a mesh axis runs over, the one named last changes fastest.
Arguments:
- load: float32 [3, 7, 7, 8, 32768], P(None, None, None, None, ('group', 'member')), may hold values from -6 to 6
- stiffness_dir: float32 [3, 32768], P(None, ('group', 'member')), may hold values from 0.5 to 4
- bulk_ratio: float32 [32768], P(('group', 'member')), may hold values from 0 to 2
- thermal_shift: float32 [32768], P(('group', 'member')), may hold values from 0.5 to 5
- contact: int32 [2, 7, 7, 32768], P(None, None, None, ('group', 'member')), may hold values 0 or 1
- loop_tie: float32 [32768], P(('group', 'member')), may hold values from 0.5 to 4
Outputs:
- solution: float32 [3, 7, 7, 8, 32768], P(None, None, None, None, ('group', 'member'))
- residual: float32 [3, 7, 7, 8, 32768], P(None, None, None, None, ('group', 'member'))
The draws below stay inside these ranges and needn't reach their ends.
All inputs are finite; a program needn't handle non-finite values. No bound on the sum of `contact` on one device may be relied on, other than what follows from the above.
Results may differ from the reference program's by a relative error of at most 0.0003.
Values sent between devices are 32-bit elements; how exact they have to be, the bound alone decides.
A program may use at most 128 MiB of HBM per device.

```python
import math
import jax
import jax.numpy as jnp
import numpy as np
from jax import lax

NODES = 8
MID_NODES = 4
COARSE_NODES = 2
SWEEPS = 2
CHEB = 6
E_DEV = 128
OWNED = 7
ELEMS = 32768
N_GROUP = 4
N_MEMBER = 64


def place_ends(entries, own_key, low, high):
    extent = entries.shape
    index_at = [jax.random.randint(jax.random.fold_in(own_key, axis), (), 0, extent[axis]) for axis in range(len(extent))]
    entries = entries.at[tuple(index_at)].set(low)
    longest = extent.index(max(extent))
    index_at[longest] = (index_at[longest] + 1) % extent[longest]
    return entries.at[tuple(index_at)].set(high)


def level_of(stream_key, extent, pieces, low, top_value):
    def one(dim, parts):
        heights = jax.random.uniform(jax.random.fold_in(jax.random.fold_in(stream_key, 6), dim), (parts,), jnp.float32, low / len(pieces), top_value / len(pieces))
        return jnp.repeat(jnp.exp(heights), extent[dim] // parts).reshape((-1,) + (1,) * (len(extent) - dim - 1))

    gain = one(*pieces[0])
    for cut in pieces[1:]:
        gain = gain * one(*cut)
    return gain


def noise(stream_key, shape, spread, limit, split=(), dtype=jnp.bfloat16):
    entries = spread * jax.random.normal(stream_key, shape, jnp.float32)
    if split:
        entries = entries * level_of(stream_key, shape, split, -0.22, 0.18)
    return jnp.clip(entries, -limit, limit).astype(dtype)


def setup_inputs(seed: int = 0) -> dict:
    streams_of = jax.random.split(jax.random.key(seed), 7)
    load = noise(streams_of[0], (3, OWNED, OWNED, NODES, ELEMS), 1.0, 6.0, ((4, 256),), jnp.float32)
    stiffness_dir = jnp.clip(jnp.exp(math.log(4.0) - 2.0794415 * jax.random.uniform(streams_of[1], (3, ELEMS), jnp.float32) ** level_of(streams_of[1], (3, ELEMS), ((1, 256),), -0.2, 0.2)), 0.5, 4.0)
    bulk_ratio = jnp.clip(2.0 * jax.random.uniform(streams_of[2], (ELEMS,), jnp.float32) ** level_of(streams_of[2], (ELEMS,), ((0, 256),), -0.2, 0.2), 0.0, 2.0)
    thermal_shift = jnp.clip(jnp.exp(math.log(5.0) - 2.3025851 * jax.random.uniform(streams_of[3], (ELEMS,), jnp.float32) ** level_of(streams_of[3], (ELEMS,), ((0, 256),), -0.2, 0.2)), 0.5, 5.0)
    contact = place_ends((jax.random.randint(streams_of[4], (2, OWNED, OWNED, ELEMS), 0, 3) < 1).astype(jnp.int32), jax.random.fold_in(streams_of[4], 1), 0, 1)
    loop_tie = jnp.clip(jnp.exp(math.log(4.0) - 2.0794415 * jax.random.uniform(streams_of[5], (ELEMS,), jnp.float32) ** level_of(streams_of[5], (ELEMS,), ((0, 256),), -0.2, 0.2)), 0.5, 4.0)
    return {"load": load, "stiffness_dir": stiffness_dir, "bulk_ratio": bulk_ratio, "thermal_shift": thermal_shift, "contact": contact, "loop_tie": loop_tie}


OMEGA = 0.3
LOWER_BOUND = 0.3
UPPER_BOUND = 3.0
HIGHEST = lax.Precision.HIGHEST


def tables(resolution):
    indices = np.arange(resolution)
    points = -np.cos(np.pi * indices / (resolution - 1))
    padded = np.concatenate([points[:1], points, points[-1:]])
    weights = (padded[2:] - padded[:-2]) / 2.0
    factor = np.where((indices == 0) | (indices == resolution - 1), 2.0, 1.0)
    spacing = points[:, None] - points[None, :] + np.eye(resolution)
    parity = np.where((indices[:, None] + indices[None, :]) % 2 == 0, 1.0, -1.0)
    offdiag = (1.0 - np.eye(resolution)) * factor[:, None] / factor[None, :] * parity / spacing
    derivative = offdiag - np.eye(resolution) * offdiag.sum(axis=1)[:, None]
    stiffness = (weights[:, None] * derivative * derivative).sum(axis=0)
    return points, weights, derivative, stiffness


def interpolation(fine_count, coarse_count):
    fine_points = tables(fine_count)[0]
    coarse_points = tables(coarse_count)[0]
    columns = []
    for column in range(coarse_count):
        values = np.ones(fine_count)
        for partner in range(coarse_count):
            if partner != column:
                values = values * (fine_points - coarse_points[partner]) / (coarse_points[column] - coarse_points[partner])
        columns.append(values)
    return jnp.asarray(np.stack(columns, axis=1), jnp.float32)


def cube_shape(resolution, extra):
    return (resolution, resolution, resolution) + (1,) * extra


def tensor(first, second, third, resolution, extra):
    return (first[:, None, None] * second[None, :, None] * third[None, None, :]).reshape(cube_shape(resolution, extra))


def element_apply(displace, coefficients, resolution):
    moduli, bulk, reaction = coefficients
    weight = jnp.asarray(tables(resolution)[1], jnp.float32)
    matrix = jnp.asarray(tables(resolution)[2], jnp.float32)
    volume = tensor(weight, weight, weight, resolution, displace.ndim - 4)
    mixed = displace + bulk * jnp.sum(displace, axis=0, keepdims=True) / 3.0
    result = reaction * volume * displace
    first = jnp.einsum("ai,cijk...->cajk...", matrix, mixed, precision=HIGHEST)
    result = result + jnp.einsum("ai,cajk...->cijk...", matrix, moduli[0] * volume * first, precision=HIGHEST)
    second = jnp.einsum("aj,cijk...->ciak...", matrix, mixed, precision=HIGHEST)
    result = result + jnp.einsum("aj,ciak...->cijk...", matrix, moduli[1] * volume * second, precision=HIGHEST)
    third = jnp.einsum("ak,cijk...->cija...", matrix, mixed, precision=HIGHEST)
    result = result + jnp.einsum("ak,cija...->cijk...", matrix, moduli[2] * volume * third, precision=HIGHEST)
    return result


def element_diagonal(coefficients, resolution):
    moduli, bulk, reaction = coefficients
    weight = jnp.asarray(tables(resolution)[1], jnp.float32)
    stiffness = jnp.asarray(tables(resolution)[3], jnp.float32)
    extra = bulk.ndim
    value = (1.0 + bulk / 3.0) * (moduli[0] * tensor(stiffness, weight, weight, resolution, extra) + moduli[1] * tensor(weight, stiffness, weight, resolution, extra) + moduli[2] * tensor(weight, weight, stiffness, resolution, extra)) + reaction * tensor(weight, weight, weight, resolution, extra)
    return jnp.broadcast_to(value[None], (3,) + value.shape)


def extend(owned, moves):
    along_next, across_next, along_prev, across_prev = moves
    layer = along_next(owned[:, 0])
    wider = jnp.concatenate([owned, layer[:, None]], axis=1)
    column = across_next(wider[:, :, 0])
    return jnp.concatenate([wider, column[:, :, None]], axis=2)


def fold(full, moves):
    along_next, across_next, along_prev, across_prev = moves
    boundary = full.shape[2] - 1
    folded = jnp.concatenate([full[:, :, :1] + across_prev(full[:, :, boundary])[:, :, None], full[:, :, 1:boundary]], axis=2)
    return jnp.concatenate([folded[:, :1] + along_prev(folded[:, boundary])[:, None], folded[:, 1:boundary]], axis=1)


def level_apply(owned, coefficients, resolution, moves):
    return fold(element_apply(extend(owned, moves), coefficients, resolution), moves)


def level_diagonal(coefficients, resolution, moves):
    return fold(element_diagonal(coefficients, resolution), moves)


def prolong(coarse, matrix, moves):
    full = extend(coarse, moves)
    full = jnp.einsum("fi,cijk...->cfjk...", matrix, full, precision=HIGHEST)
    full = jnp.einsum("fj,cijk...->cifk...", matrix, full, precision=HIGHEST)
    full = jnp.einsum("fk,cijk...->cijf...", matrix, full, precision=HIGHEST)
    boundary = matrix.shape[0] - 1
    return full[:, :boundary, :boundary]


def restrict(fine, matrix, moves):
    wider = jnp.concatenate([fine, jnp.zeros_like(fine[:, :1])], axis=1)
    full = jnp.concatenate([wider, jnp.zeros_like(wider[:, :, :1])], axis=2)
    full = jnp.einsum("fi,cfjk...->cijk...", matrix, full, precision=HIGHEST)
    full = jnp.einsum("fj,cifk...->cijk...", matrix, full, precision=HIGHEST)
    full = jnp.einsum("fk,cijf...->cijk...", matrix, full, precision=HIGHEST)
    return fold(full, moves)


def free_mask(contact_float, resolution):
    middle = jnp.ones(contact_float.shape[1:3] + (resolution - 2,) + contact_float.shape[3:], jnp.float32)
    return jnp.concatenate([(1.0 - contact_float[0])[:, :, None], middle, (1.0 - contact_float[1])[:, :, None]], axis=2)


def smooth(iterate, rhs, operator, inverse, sweeps):
    for repeat in range(sweeps):
        iterate = iterate + OMEGA * inverse * (rhs - operator(iterate))
    return iterate


def chebyshev(rhs, operator, inverse):
    center = 0.5 * (UPPER_BOUND + LOWER_BOUND)
    radius = 0.5 * (UPPER_BOUND - LOWER_BOUND)
    ratio = center / radius
    damping_now = 1.0 / ratio
    remain = rhs
    update = inverse * remain / center
    iterate = jnp.zeros_like(rhs)
    for iteration in range(CHEB):
        iterate = iterate + update
        if iteration + 1 < CHEB:
            remain = remain - operator(update)
            damping_next = 1.0 / (2.0 * ratio - damping_now)
            update = damping_next * damping_now * update + (2.0 * damping_next / radius) * inverse * remain
            damping_now = damping_next
    return iterate


def vcycle(load, coefficients, freedom, moves, coarse_solve):
    fine_mid = interpolation(NODES, MID_NODES)
    mid_coarse = interpolation(MID_NODES, COARSE_NODES)

    def apply_fine(values):
        return freedom * level_apply(values, coefficients, NODES, moves)

    def apply_mid(values):
        return level_apply(values, coefficients, MID_NODES, moves)

    inverse_fine = freedom / level_diagonal(coefficients, NODES, moves)
    inverse_mid = 1.0 / level_diagonal(coefficients, MID_NODES, moves)
    rhs_fine = freedom * load
    fine_iter = smooth(OMEGA * inverse_fine * rhs_fine, rhs_fine, apply_fine, inverse_fine, SWEEPS - 1)
    rhs_mid = restrict(rhs_fine - apply_fine(fine_iter), fine_mid, moves)
    mid_iter = smooth(OMEGA * inverse_mid * rhs_mid, rhs_mid, apply_mid, inverse_mid, SWEEPS - 1)
    rhs_coarse = restrict(rhs_mid - apply_mid(mid_iter), mid_coarse, moves)
    coarse_iter = coarse_solve(rhs_coarse)
    mid_iter = smooth(mid_iter + prolong(coarse_iter, mid_coarse, moves), rhs_mid, apply_mid, inverse_mid, SWEEPS)
    fine_iter = smooth(fine_iter + freedom * prolong(mid_iter, fine_mid, moves), rhs_fine, apply_fine, inverse_fine, SWEEPS)
    return fine_iter, rhs_fine - apply_fine(fine_iter)


def loop_shift(values, upward):
    axis = values.ndim - 3
    zeros = jnp.zeros_like(lax.slice_in_dim(values, 0, 1, axis=axis))
    if upward:
        return jnp.concatenate([lax.slice_in_dim(values, 1, N_GROUP, axis=axis), zeros], axis=axis)
    return jnp.concatenate([zeros, lax.slice_in_dim(values, 0, N_GROUP - 1, axis=axis)], axis=axis)


def reference(load, stiffness_dir, bulk_ratio, thermal_shift, contact, loop_tie):
    layout = (N_GROUP, N_MEMBER, E_DEV)

    def cells(values):
        return values.reshape(values.shape[:-1] + layout)

    def along_next(values):
        return jnp.roll(values, -1, axis=-2)

    def along_prev(values):
        return jnp.roll(values, 1, axis=-2)

    def across_next(values):
        return jnp.roll(values, -1, axis=-1)

    def across_prev(values):
        return jnp.roll(values, 1, axis=-1)

    moves = (along_next, across_next, along_prev, across_prev)
    coefficients = (cells(stiffness_dir), cells(bulk_ratio), cells(thermal_shift))
    freedom = free_mask(cells(contact).astype(jnp.float32), NODES)
    loop_index = lax.broadcasted_iota(jnp.int32, layout, 0)
    tie_live = jnp.where(loop_index < N_GROUP - 1, cells(loop_tie), jnp.float32(0.0))
    tie_under = loop_shift(tie_live, False)

    def apply_coarse(values):
        return level_apply(values, coefficients, COARSE_NODES, moves) + tie_live * (values - loop_shift(values, True)) + tie_under * (values - loop_shift(values, False))

    inverse_coarse = 1.0 / (level_diagonal(coefficients, COARSE_NODES, moves) + tie_live + tie_under)

    def coarse_solve(rhs):
        return chebyshev(rhs, apply_coarse, inverse_coarse)

    solution, residual = vcycle(cells(load), coefficients, freedom, moves, coarse_solve)
    return solution.reshape(load.shape), residual.reshape(load.shape)
```

```python
import functools

import jax
import jax.numpy as jnp
import numpy as np
from jax import lax
from jax.experimental import pallas as pl
from jax.experimental.pallas import tpu as pltpu
from jax.sharding import PartitionSpec as P

NODES = 8
MID_NODES = 4
COARSE_NODES = 2
SWEEPS = 2
CHEB = 6

OMEGA = 0.3
LOWER_BOUND = 0.3
UPPER_BOUND = 3.0
MESH = pl.DeviceIdType.MESH
LANES = 128
SUB = 8


def tables(resolution):
    indices = np.arange(resolution)
    points = -np.cos(np.pi * indices / (resolution - 1))
    padded = np.concatenate([points[:1], points, points[-1:]])
    weights = (padded[2:] - padded[:-2]) / 2.0
    factor = np.where((indices == 0) | (indices == resolution - 1), 2.0, 1.0)
    spacing = points[:, None] - points[None, :] + np.eye(resolution)
    parity = np.where((indices[:, None] + indices[None, :]) % 2 == 0, 1.0, -1.0)
    offdiag = (1.0 - np.eye(resolution)) * factor[:, None] / factor[None, :] * parity / spacing
    derivative = offdiag - np.eye(resolution) * offdiag.sum(axis=1)[:, None]
    stiffness = (weights[:, None] * derivative * derivative).sum(axis=0)
    return (points, weights, derivative, stiffness)


def interpolation(fine_count, coarse_count):
    fine_points = tables(fine_count)[0]
    coarse_points = tables(coarse_count)[0]
    columns = []
    for column in range(coarse_count):
        values = np.ones(fine_count)
        for partner in range(coarse_count):
            if partner != column:
                values = (
                    values
                    * (fine_points - coarse_points[partner])
                    / (coarse_points[column] - coarse_points[partner])
                )
        columns.append(values)
    return np.stack(columns, axis=1)


class Columns:
    def __init__(self):
        self.rows, self.index = [], {}

    def add(self, column):
        column = np.asarray(column, np.float32)
        key = tuple(column.tolist())
        if key not in self.index:
            self.index[key] = len(self.rows)
            self.rows.append(column)
        return self.index[key]

    def matrix(self, values):
        full = np.zeros((SUB, SUB))
        full[: values.shape[0], : values.shape[1]] = values
        terms = []
        for shift in range(SUB):
            column = [full[s, (s - shift) % SUB] for s in range(SUB)]
            if np.any(column):
                terms.append((shift, self.add(column)))
        return terms

    def table(self):
        return np.repeat(np.stack(self.rows)[:, :, None], LANES, axis=2)


def padded(values):
    return np.concatenate([values, np.zeros(SUB - len(values))])


def make_plan():
    cols = Columns()
    plan = {}
    for n in (NODES, MID_NODES):
        _, w, d, g = tables(n)
        hat = (d.T @ np.diag(w) @ d) / w[:, None]
        plan[n] = dict(
            n=n, w=w, g=g, hat=hat, along=cols.matrix(hat), wk=cols.add(padded(w)), gk=cols.add(padded(g)),
        )
    pad = np.ones(SUB)
    pad[:MID_NODES] = 0.0
    plan["pad_mid"] = cols.add(pad)
    first, last = np.zeros(SUB), np.zeros(SUB)
    first[0], last[SUB - 1] = 1.0, 1.0
    plan["first"], plan["last"] = cols.add(first), cols.add(last)
    jf = interpolation(NODES, MID_NODES)
    jc = interpolation(MID_NODES, COARSE_NODES)
    plan["jf"], plan["jc"] = jf, jc
    plan["jf_up"], plan["jf_down"] = cols.matrix(jf), cols.matrix(jf.T)
    low = np.zeros(SUB)
    low[:MID_NODES] = 1.0
    plan["low"] = cols.add(low)
    down, up = [], []
    for c in range(3):
        m = np.zeros((SUB, SUB))
        m[2 * c : 2 * c + 2, :MID_NODES] = jc.T
        down.append(cols.matrix(m))
        m = np.zeros((SUB, SUB))
        m[:MID_NODES, 2 * c : 2 * c + 2] = jc
        up.append(cols.matrix(m))
    plan["jc_down"], plan["jc_up"] = down, up
    m = np.zeros((SUB, SUB))
    swap = np.zeros((SUB, SUB))
    for c in range(3):
        for k in range(2):
            swap[2 * c + k, 2 * c + 1 - k] = 1.0
            for e in range(3):
                m[2 * c + k, 2 * e + k] = 1.0
    plan["csum"], plan["kswap"] = cols.matrix(m), cols.matrix(swap)
    return plan, cols.table()


PLAN, TABLE = make_plan()


def lane_up(x):
    return pltpu.roll(x, 1, x.ndim - 1)


def lane_down(x):
    return pltpu.roll(x, LANES - 1, x.ndim - 1)


def weigh(scalars, arrays):
    total = None
    for s, x in zip(scalars, arrays):
        s = float(s)
        if s == 0.0:
            continue
        term = x if s == 1.0 else x * s
        total = term if total is None else total + term
    return total


def sublanes(x, terms, tab):
    total = None
    for shift, column in terms:
        moved = x if shift == 0 else pltpu.roll(x, shift, x.ndim - 2)
        term = moved * tab[column]
        total = term if total is None else total + term
    return total


def split(matrix, a):
    n = matrix.shape[0]
    half = n // 2
    even = [(matrix[a, j] + matrix[a, n - 1 - j]) / 2 for j in range(half)]
    odd = [(matrix[a, j] - matrix[a, n - 1 - j]) / 2 for j in range(half)]
    return even, odd


def centro(matrix, xs):
    n = matrix.shape[0]
    half = n // 2
    es = [xs[j] + xs[n - 1 - j] for j in range(half)]
    os = [xs[j] - xs[n - 1 - j] for j in range(half)]
    out = [None] * n
    for a in range(half):
        even, odd = split(matrix, a)
        p, q = weigh(even, es), weigh(odd, os)
        out[a], out[n - 1 - a] = p + q, p - q
    return out


def kernel(
    load, stiff, bulk, shift, contact, tie, tab,
    sol, res,
    X, V, EO, B0, FD, FM, RB, G,
    X1, B1, ID1,
    CO, pack, pack_prev, pack_next, pack_under, pack_under_next,
    load_next, contact_next,
    f_up, f_dn, f_from_prev, f_from_next,
    m_up, m_dn, m_from_prev, m_from_next,
    c_up, c_dn, c_from_prev, c_from_next,
    d_out, d_above, d_below,
    send, recv, gsend, grecv,
):
    p8, p4 = PLAN[NODES], PLAN[MID_NODES]
    w8, w4 = p8["w"], p4["w"]
    g = lax.axis_index("group")
    m = lax.axis_index("member")
    loops, members = lax.axis_size("group"), lax.axis_size("member")
    nxt, prv = lax.rem(m + 1, members), lax.rem(m + members - 1, members)
    has_above, has_below = g < loops - 1, g > 0
    slot = [0]
    pending = []

    def to_member(src, dst, target):
        i = slot[0]
        slot[0] += 1
        copy = pltpu.make_async_remote_copy(
            src_ref=src, dst_ref=dst, send_sem=send.at[i], recv_sem=recv.at[i],
            device_id={"member": target}, device_id_type=MESH,
        )
        copy.start()
        pending.append(copy)
        return copy

    gslot = [0]
    gpending = []

    def to_groups(up, down):
        made = []
        for pair, exists, comes, target in (
            (up, has_above, has_below, g + 1), (down, has_below, has_above, g - 1),
        ):
            if pair is None:
                continue
            i = gslot[0]
            gslot[0] += 1
            copy = pltpu.make_async_remote_copy(
                src_ref=pair[0], dst_ref=pair[1], send_sem=gsend.at[i], recv_sem=grecv.at[i],
                device_id={"group": target}, device_id_type=MESH,
            )
            pl.when(exists)(copy.start)
            gpending.append((exists, copy))
            made.append((comes, copy))

        def arrive():
            for comes, copy in made:
                pl.when(comes)(copy.wait_recv)

        return arrive

    pack_under[...] = jnp.zeros((SUB, LANES), jnp.float32)
    d_above[...] = jnp.zeros(d_above.shape, jnp.float32)
    d_below[...] = jnp.zeros(d_below.shape, jnp.float32)
    barrier = pltpu.get_barrier_semaphore()
    for target in (nxt, prv):
        pl.semaphore_signal(barrier, inc=1, device_id={"member": target}, device_id_type=MESH)

    @pl.when(has_above)
    def _():
        pl.semaphore_signal(barrier, inc=1, device_id={"group": g + 1}, device_id_type=MESH)

    @pl.when(has_below)
    def _():
        pl.semaphore_signal(barrier, inc=1, device_id={"group": g - 1}, device_id_type=MESH)

    pack[...] = jnp.concatenate(
        [stiff[...], bulk[...], shift[...], tie[...], jnp.zeros((2, LANES), jnp.float32)], axis=0
    )
    pl.semaphore_wait(barrier, 2 + has_above.astype(jnp.int32) + has_below.astype(jnp.int32))

    setup = [
        to_member(pack, pack_prev, nxt),
        to_member(pack, pack_next, prv),
        to_member(contact.at[:, 0], contact_next, prv),
        to_member(load.at[:, 0], load_next, prv),
    ]
    under_arrives = to_groups((pack, pack_under), None)

    def row(ref, i):
        return jnp.broadcast_to(ref[i : i + 1, :], (SUB, LANES))

    def quantities(ref):
        scale = 1.0 + row(ref, 3) * (1.0 / 3.0)
        return [scale * row(ref, 0), scale * row(ref, 1), scale * row(ref, 2), row(ref, 4)]

    third = row(pack, 3) * (1.0 / 3.0)
    CO[0] = third
    for base, plan in ((1, p8), (5, p4)):
        wk = tab[plan["wk"]]
        CO[base] = row(pack, 4) * wk
        for d in range(3):
            CO[base + 1 + d] = row(pack, d) * wk

    own_q = quantities(pack)

    def diagonal(plan, q, a, b):
        w, gg = plan["w"], plan["g"]
        wk, gk = tab[plan["wk"]], tab[plan["gk"]]
        inner = q[0] * float(gg[a] * w[b]) + q[1] * float(w[a] * gg[b]) + q[3] * float(w[a] * w[b])
        return inner * wk + q[2] * gk * float(w[a] * w[b])

    def edge(q):
        return [x + lane_up(x) for x in q]

    def fine_masks(a, lower, upper, q):
        qe = edge(q)
        for b in range(NODES - 1):
            low = jnp.broadcast_to(lower[b : b + 1, :].astype(jnp.float32), (SUB, LANES))
            high = jnp.broadcast_to(upper[b : b + 1, :].astype(jnp.float32), (SUB, LANES))
            free = 1.0 - low * tab[PLAN["first"]] - high * tab[PLAN["last"]]
            FM[a, b] = free
            FD[a, b] = OMEGA * free / diagonal(p8, qe if b == 0 else q, a, b)

    def start_x(c, a, values):
        rhs = FM[a] * values
        B0[c, a] = rhs
        x = FD[a] * rhs
        X[c, a, 0 : NODES - 1] = x
        X[c, a, NODES - 1] = lane_down(x[0])

    for a in range(1, NODES - 1):
        fine_masks(a, contact.at[0, a], contact.at[1, a], own_q)

    @pl.loop(0, 3)
    def _(c):
        for a in range(1, NODES - 1):
            start_x(c, a, load[c, a])

    for copy in setup[:3]:
        copy.wait_recv()
    prev_q = [x + y for x, y in zip(own_q, quantities(pack_prev))]
    next_q = [x + y for x, y in zip(own_q, quantities(pack_next))]
    fine_masks(0, contact.at[0, 0], contact.at[1, 0], prev_q)
    fine_masks(NODES - 1, contact_next.at[0], contact_next.at[1], next_q)
    setup[3].wait_recv()

    @pl.loop(0, 3)
    def _(c):
        start_x(c, 0, load[c, 0])
        start_x(c, NODES - 1, load_next[c])

    last8 = NODES - 1

    def fine_prepare():
        for j in range(NODES // 2):
            k = last8 - j
            tj = CO[0] * (X[0, j] + X[1, j] + X[2, j])
            tk = CO[0] * (X[0, k] + X[1, k] + X[2, k])
            for c in range(3):
                vj, vk = X[c, j] + tj, X[c, k] + tk
                V[c, j], V[c, k] = vj, vk
                EO[c, j], EO[c, NODES // 2 + j] = vj + vk, vj - vk

    def fine_pair(c, a, planes=None):
        even, odd = split(p8["hat"], a)
        p = weigh(even, [EO[c, j] for j in range(NODES // 2)])
        q = weigh(odd, [EO[c, NODES // 2 + j] for j in range(NODES // 2)])
        out = []
        for plane, ya in ((a, p + q), (last8 - a, p - q)):
            v = V[c, plane]
            yk = sublanes(v, p8["along"], tab)
            base = CO[1] * X[c, plane] + CO[2] * ya + CO[4] * yk
            yb = centro(p8["hat"], [v[b] for b in range(NODES)])
            rows = [
                (base[b] + CO[3] * yb[b]) * float(w8[plane] * w8[b]) for b in range(NODES)
            ]
            rows[0] = rows[0] + lane_up(rows[last8])
            out.append(jnp.stack(rows[:last8], axis=0))
        return out

    def fine_update(c, a, z):
        x = X[c, a, 0:last8] + FD[a] * (B0[c, a] - z)
        X[c, a, 0:last8] = x
        X[c, a, last8] = lane_down(x[0])

    def fine_sweep(i, meanwhile=None):
        fine_prepare()

        @pl.loop(0, 3)
        def _(c):
            z = fine_pair(c, 0)
            f_dn[i, c], f_up[i, c] = z[0], z[1]

        up = to_member(f_up.at[i], f_from_prev.at[i], nxt)
        down = to_member(f_dn.at[i], f_from_next.at[i], prv)

        @pl.loop(0, 3)
        def _(c):
            for a in range(1, NODES // 2):
                z = fine_pair(c, a)
                fine_update(c, a, z[0])
                fine_update(c, last8 - a, z[1])

        if meanwhile is not None:
            meanwhile()
        up.wait_recv()
        down.wait_recv()

        @pl.loop(0, 3)
        def _(c):
            fine_update(c, 0, f_dn[i, c] + f_from_prev[i, c])
            fine_update(c, last8, f_up[i, c] + f_from_next[i, c])

    last4 = MID_NODES - 1
    coarse_data = {}

    def mid_setup():
        under_arrives()
        coarse_data["under"] = to_member(pack_under, pack_under_next, prv)
        pad = tab[PLAN["pad_mid"]]
        for a in range(MID_NODES):
            q = prev_q if a == 0 else next_q if a == last4 else own_q
            qe = edge(q)
            for b in range(last4):
                ID1[a, b] = OMEGA / (diagonal(p4, qe if b == 0 else q, a, b) + pad)

    low = tab[PLAN["low"]]

    def bundle(z):
        tiles = [z[c, b] for c in range(3) for b in range(last4)]
        rows = [tiles[2 * i] + pltpu.roll(tiles[2 * i + 1], 4, 0) for i in range(4)]
        return jnp.stack(rows + [tiles[8]], axis=0)

    def unbundle(rows):
        tiles = []
        for i in range(4):
            tiles.append(rows[i] * low)
            tiles.append(pltpu.roll(rows[i], 4, 0) * low)
        tiles.append(rows[4])
        return jnp.stack([jnp.stack(tiles[3 * c : 3 * c + 3], axis=0) for c in range(3)], axis=0)

    def mid_apply():
        us = [X1[a] for a in range(MID_NODES)]
        vs = [u + CO[0] * jnp.sum(u, axis=0, keepdims=True) for u in us]
        yas = centro(p4["hat"], vs)
        out = []
        for a in range(MID_NODES):
            yk = sublanes(vs[a], p4["along"], tab)
            base = CO[5] * us[a] + CO[6] * yas[a] + CO[8] * yk
            yb = centro(p4["hat"], [vs[a][:, b] for b in range(MID_NODES)])
            rows = [
                (base[:, b] + CO[7] * yb[b]) * float(w4[a] * w4[b]) for b in range(MID_NODES)
            ]
            rows[0] = rows[0] + lane_up(rows[last4])
            out.append(jnp.stack(rows[:last4], axis=1))
        return out

    def mid_store(a, x):
        X1[a, :, 0:last4] = x
        X1[a, :, last4] = lane_down(x[:, 0])

    mid_slot = [0]

    def mid_exchange(low_face, high_face):
        i = mid_slot[0]
        mid_slot[0] += 1
        m_dn[i], m_up[i] = bundle(low_face), bundle(high_face)
        up = to_member(m_up.at[i], m_from_prev.at[i], nxt)
        down = to_member(m_dn.at[i], m_from_next.at[i], prv)

        def arrive():
            up.wait_recv()
            down.wait_recv()
            return unbundle(m_from_prev[i]), unbundle(m_from_next[i])

        return arrive

    def mid_sweep():
        z = mid_apply()
        arrive = mid_exchange(z[0], z[last4])

        def update(a, total):
            mid_store(a, X1[a, :, 0:last4] + ID1[a] * (B1[a] - total))

        for a in range(1, last4):
            update(a, z[a])
        below, above = arrive()
        update(0, z[0] + below)
        update(last4, z[last4] + above)

    coarse_slot = [0]

    def coarse_exchange(low_face, high_face):
        i = coarse_slot[0]
        coarse_slot[0] += 1
        c_dn[i], c_up[i] = low_face, high_face
        up = to_member(c_up.at[i], c_from_prev.at[i], nxt)
        down = to_member(c_dn.at[i], c_from_next.at[i], prv)

        def arrive():
            up.wait_recv()
            down.wait_recv()
            return c_from_prev[i], c_from_next[i]

        return arrive

    def coarse_apply(u):
        half = [row(pack, d) * 0.5 for d in range(3)]
        react = row(pack, 4)
        wide = [[x, lane_down(x)] for x in u]
        sums = [sublanes(x, PLAN["csum"], tab) for x in u]
        vs = [
            [wide[a][0] + third * sums[a], wide[a][1] + third * lane_down(sums[a])] for a in range(2)
        ]
        out = []
        for a in range(2):
            rows = []
            for b in range(2):
                v = vs[a][b]
                rows.append(
                    react * wide[a][b]
                    + half[0] * (v - vs[1 - a][b])
                    + half[1] * (v - vs[a][1 - b])
                    + half[2] * (v - sublanes(v, PLAN["kswap"], tab))
                )
            out.append(rows[0] + lane_up(rows[1]))
        return out

    fine_sweep(0, mid_setup)

    jf, jc = PLAN["jf"], PLAN["jc"]
    fine_prepare()

    @pl.loop(0, 3)
    def _(c):
        for a in range(NODES // 2):
            z = fine_pair(c, a)
            for plane, value in ((a, z[0]), (last8 - a, z[1])):
                r = FM[plane] * value
                r = -r if plane == last8 else B0[c, plane] - r
                for bc in range(MID_NODES):
                    RB[plane, bc] = weigh(jf[:last8, bc], [r[b] for b in range(last8)])
        for plane in range(NODES):
            RB[plane, 0] = RB[plane, 0] + lane_up(RB[plane, last4])
        for ac in range(MID_NODES):
            part = weigh(jf[:, ac], [RB[a, 0:last4] for a in range(NODES)])
            G[ac, c] = sublanes(part, PLAN["jf_down"], tab)

    arrive = mid_exchange(G[0], G[last4])
    for a in range(1, last4):
        B1[a] = G[a]
        mid_store(a, ID1[a] * G[a])
    tie_own = row(pack, 5)
    tie_next = row(pack_next, 5)
    live = has_above.astype(jnp.float32)
    under = has_below.astype(jnp.float32)
    coarse_data["under"].wait_recv()
    ties = [tie_own * live, tie_next * live]
    ties_under = [row(pack_under, 5) * under, row(pack_under_next, 5) * under]
    inv2 = []
    for q, t, tu in zip((prev_q, next_q), ties, ties_under):
        qe = edge(q)
        diag = (qe[0] + qe[1] + qe[2]) * 0.5 + qe[3]
        inv2.append(1.0 / (diag + t + tu))
    below, above = arrive()
    for a, extra in ((0, below), (last4, above)):
        b1 = G[a] + extra
        B1[a] = b1
        mid_store(a, ID1[a] * b1)

    mid_sweep()
    z = mid_apply()
    rs = [B1[a] - z[a] for a in range(last4)] + [-z[last4]]
    hs = []
    for ac in range(2):
        part = weigh(jc[:, ac], rs)
        along = [weigh(jc[:last4, bc], [part[:, b] for b in range(last4)]) for bc in range(2)]
        along = along[0] + lane_up(along[1])
        total = None
        for c in range(3):
            term = sublanes(along[c], PLAN["jc_down"][c], tab)
            total = term if total is None else total + term
        hs.append(total)
    arrive = coarse_exchange(hs[0], hs[1])
    below, above = arrive()
    remain = [hs[0] + below, hs[1] + above]

    center = 0.5 * (UPPER_BOUND + LOWER_BOUND)
    radius = 0.5 * (UPPER_BOUND - LOWER_BOUND)
    ratio = center / radius
    damping_now = 1.0 / ratio
    update = [inv2[a] * remain[a] * (1.0 / center) for a in range(2)]
    x2 = [jnp.zeros((SUB, LANES), jnp.float32)] * 2
    for iteration in range(CHEB):
        x2 = [x + d for x, d in zip(x2, update)]
        if iteration + 1 < CHEB:
            for a in range(2):
                d_out[iteration, a] = update[a]
            groups_arrive = to_groups(
                (d_out.at[iteration], d_below.at[iteration]),
                (d_out.at[iteration], d_above.at[iteration]),
            )
            z = coarse_apply(update)
            arrive = coarse_exchange(z[0], z[1])
            damping_next = 1.0 / (2.0 * ratio - damping_now)
            groups_arrive()
            partial = [
                remain[a]
                - z[a]
                - ties[a] * (update[a] - d_above[iteration, a])
                - ties_under[a] * (update[a] - d_below[iteration, a])
                for a in range(2)
            ]
            below, above = arrive()
            remain = [partial[0] - below, partial[1] - above]
            update = [
                (damping_next * damping_now) * update[a]
                + (2.0 * damping_next / radius) * inv2[a] * remain[a]
                for a in range(2)
            ]
            damping_now = damping_next

    wide = [[x, lane_down(x)] for x in x2]
    lifted = []
    for a in range(2):
        lifted.append(
            [
                jnp.stack([sublanes(wide[a][b], PLAN["jc_up"][c], tab) for c in range(3)], axis=0)
                for b in range(2)
            ]
        )
    for a in range(MID_NODES):
        cross = [weigh(jc[a], [lifted[0][b], lifted[1][b]]) for b in range(2)]
        add = jnp.stack([weigh(jc[b], cross) for b in range(last4)], axis=1)
        mid_store(a, X1[a, :, 0:last4] + add)
    mid_sweep()
    mid_sweep()

    @pl.loop(0, 3)
    def _(c):
        for a in range(MID_NODES):
            RB[a] = sublanes(X1[a, c], PLAN["jf_up"], tab)
        for a in range(NODES):
            part = weigh(jf[a], [RB[i] for i in range(MID_NODES)])
            add = jnp.stack(
                [weigh(jf[b], [part[i] for i in range(MID_NODES)]) for b in range(last8)], axis=0
            )
            x = X[c, a, 0:last8] + FM[a] * add
            X[c, a, 0:last8] = x
            X[c, a, last8] = lane_down(x[0])

    fine_sweep(1)
    fine_sweep(2)

    fine_prepare()

    @pl.loop(0, 3)
    def _(c):
        z = fine_pair(c, 0)
        f_dn[3, c], f_up[3, c] = z[0], z[1]

    final = to_member(f_up.at[3], f_from_prev.at[3], nxt)

    @pl.loop(0, 3)
    def _(c):
        for a in range(1, NODES // 2):
            z = fine_pair(c, a)
            res[c, a] = B0[c, a] - FM[a] * z[0]
            res[c, last8 - a] = B0[c, last8 - a] - FM[last8 - a] * z[1]
        for a in range(last8):
            sol[c, a] = X[c, a, 0:last8]

    final.wait_recv()

    @pl.loop(0, 3)
    def _(c):
        res[c, 0] = B0[c, 0] - FM[0] * (f_dn[3, c] + f_from_prev[3, c])

    for copy in pending:
        copy.wait_send()
    for exists, copy in gpending:
        pl.when(exists)(copy.wait_send)


def body(load, stiffness_dir, bulk_ratio, thermal_shift, contact, loop_tie):
    f32 = jnp.float32
    n, q, o = NODES, MID_NODES, NODES - 1
    tile = (SUB, LANES)

    def vmem(*shape):
        return pltpu.VMEM(shape, f32)

    spec = pl.BlockSpec(memory_space=pltpu.VMEM)
    member_slots, group_slots = 40, 12
    scratch = [
        vmem(3, n, n, *tile), vmem(3, n, n, *tile), vmem(3, n, n, *tile),
        vmem(3, n, o, *tile), vmem(n, o, *tile), vmem(n, o, *tile),
        vmem(n, q, *tile), vmem(q, 3, q - 1, *tile),
        vmem(q, 3, q, *tile), vmem(q, 3, q - 1, *tile), vmem(q, q - 1, *tile),
        vmem(9, *tile),
        vmem(*tile), vmem(*tile), vmem(*tile), vmem(*tile), vmem(*tile),
        vmem(3, o, *tile), pltpu.VMEM((2, o, LANES), jnp.int32),
    ]
    scratch += [vmem(4, 3, o, *tile) for _ in range(4)]
    scratch += [vmem(4, 5, *tile) for _ in range(4)]
    scratch += [vmem(6, *tile) for _ in range(4)]
    scratch += [vmem(5, 2, *tile) for _ in range(3)]
    scratch += [
        pltpu.SemaphoreType.DMA((member_slots,)),
        pltpu.SemaphoreType.DMA((member_slots,)),
        pltpu.SemaphoreType.DMA((group_slots,)),
        pltpu.SemaphoreType.DMA((group_slots,)),
    ]
    shape = jax.ShapeDtypeStruct(load.shape, f32)
    return pl.pallas_call(
        kernel,
        out_shape=(shape, shape),
        in_specs=[spec] * 7,
        out_specs=(spec, spec),
        scratch_shapes=scratch,
        compiler_params=pltpu.CompilerParams(
            collective_id=0, has_side_effects=True, vmem_limit_bytes=48 * 2**20
        ),
    )(
        load,
        stiffness_dir,
        bulk_ratio.reshape(1, LANES),
        thermal_shift.reshape(1, LANES),
        contact,
        loop_tie.reshape(1, LANES),
        jnp.asarray(TABLE),
    )


def solution(mesh):
    in_specs = (
        P(None, None, None, None, ("group", "member")),
        P(None, ("group", "member")),
        P(("group", "member")),
        P(("group", "member")),
        P(None, None, None, ("group", "member")),
        P(("group", "member")),
    )
    out_specs = (
        P(None, None, None, None, ("group", "member")),
        P(None, None, None, None, ("group", "member")),
    )
    return jax.shard_map(body, mesh=mesh, in_specs=in_specs, out_specs=out_specs, check_vma=False)
```

```python
import functools

import jax
import jax.numpy as jnp
import numpy as np
from jax import lax
from jax.experimental import pallas as pl
from jax.experimental.pallas import tpu as pltpu
from jax.sharding import PartitionSpec as P

NODES = 8
MID_NODES = 4
COARSE_NODES = 2
SWEEPS = 2
CHEB = 6

OMEGA = 0.3
LOWER_BOUND = 0.3
UPPER_BOUND = 3.0
MESH = pl.DeviceIdType.MESH
REACH = CHEB
SPAN = 2 * REACH + 1
PLANES = 2 * REACH
LANES = 128
SUB = 8


def tables(resolution):
    indices = np.arange(resolution)
    points = -np.cos(np.pi * indices / (resolution - 1))
    padded = np.concatenate([points[:1], points, points[-1:]])
    weights = (padded[2:] - padded[:-2]) / 2.0
    factor = np.where((indices == 0) | (indices == resolution - 1), 2.0, 1.0)
    spacing = points[:, None] - points[None, :] + np.eye(resolution)
    parity = np.where((indices[:, None] + indices[None, :]) % 2 == 0, 1.0, -1.0)
    offdiag = (1.0 - np.eye(resolution)) * factor[:, None] / factor[None, :] * parity / spacing
    derivative = offdiag - np.eye(resolution) * offdiag.sum(axis=1)[:, None]
    stiffness = (weights[:, None] * derivative * derivative).sum(axis=0)
    return (points, weights, derivative, stiffness)


def interpolation(fine_count, coarse_count):
    fine_points = tables(fine_count)[0]
    coarse_points = tables(coarse_count)[0]
    columns = []
    for column in range(coarse_count):
        values = np.ones(fine_count)
        for partner in range(coarse_count):
            if partner != column:
                values = (
                    values
                    * (fine_points - coarse_points[partner])
                    / (coarse_points[column] - coarse_points[partner])
                )
        columns.append(values)
    return np.stack(columns, axis=1)


class Columns:
    def __init__(self):
        self.rows, self.index = [], {}

    def add(self, column):
        column = np.asarray(column, np.float32)
        key = tuple(column.tolist())
        if key not in self.index:
            self.index[key] = len(self.rows)
            self.rows.append(column)
        return self.index[key]

    def matrix(self, values):
        full = np.zeros((SUB, SUB))
        full[: values.shape[0], : values.shape[1]] = values
        terms = []
        for shift in range(SUB):
            column = [full[s, (s - shift) % SUB] for s in range(SUB)]
            if np.any(column):
                terms.append((shift, self.add(column)))
        return terms

    def table(self):
        return np.repeat(np.stack(self.rows)[:, :, None], LANES, axis=2)


def padded(values):
    return np.concatenate([values, np.zeros(SUB - len(values))])


def make_plan():
    cols = Columns()
    plan = {}
    for n in (NODES, MID_NODES):
        _, w, d, g = tables(n)
        hat = (d.T @ np.diag(w) @ d) / w[:, None]
        plan[n] = dict(
            n=n, w=w, g=g, hat=hat, along=cols.matrix(hat), wk=cols.add(padded(w)), gk=cols.add(padded(g)),
        )
    pad = np.ones(SUB)
    pad[:MID_NODES] = 0.0
    plan["pad_mid"] = cols.add(pad)
    first, last = np.zeros(SUB), np.zeros(SUB)
    first[0], last[SUB - 1] = 1.0, 1.0
    plan["first"], plan["last"] = cols.add(first), cols.add(last)
    jf = interpolation(NODES, MID_NODES)
    jc = interpolation(MID_NODES, COARSE_NODES)
    plan["jf"], plan["jc"] = jf, jc
    plan["jf_up"], plan["jf_down"] = cols.matrix(jf), cols.matrix(jf.T)
    low = np.zeros(SUB)
    low[:MID_NODES] = 1.0
    plan["low"] = cols.add(low)
    down, up = [], []
    for c in range(3):
        m = np.zeros((SUB, SUB))
        m[2 * c : 2 * c + 2, :MID_NODES] = jc.T
        down.append(cols.matrix(m))
        m = np.zeros((SUB, SUB))
        m[:MID_NODES, 2 * c : 2 * c + 2] = jc
        up.append(cols.matrix(m))
    plan["jc_down"], plan["jc_up"] = down, up
    m = np.zeros((SUB, SUB))
    swap = np.zeros((SUB, SUB))
    for c in range(3):
        for k in range(2):
            swap[2 * c + k, 2 * c + 1 - k] = 1.0
            for e in range(3):
                m[2 * c + k, 2 * e + k] = 1.0
    plan["csum"], plan["kswap"] = cols.matrix(m), cols.matrix(swap)
    return plan, cols.table()


PLAN, TABLE = make_plan()


def lane_up(x):
    return pltpu.roll(x, 1, x.ndim - 1)


def lane_down(x):
    return pltpu.roll(x, LANES - 1, x.ndim - 1)


def weigh(scalars, arrays):
    total = None
    for s, x in zip(scalars, arrays):
        s = float(s)
        if s == 0.0:
            continue
        term = x if s == 1.0 else x * s
        total = term if total is None else total + term
    return total


def sublanes(x, terms, tab):
    total = None
    for shift, column in terms:
        moved = x if shift == 0 else pltpu.roll(x, shift, x.ndim - 2)
        term = moved * tab[column]
        total = term if total is None else total + term
    return total


def split(matrix, a):
    n = matrix.shape[0]
    half = n // 2
    even = [(matrix[a, j] + matrix[a, n - 1 - j]) / 2 for j in range(half)]
    odd = [(matrix[a, j] - matrix[a, n - 1 - j]) / 2 for j in range(half)]
    return even, odd


def centro(matrix, xs):
    n = matrix.shape[0]
    half = n // 2
    es = [xs[j] + xs[n - 1 - j] for j in range(half)]
    os = [xs[j] - xs[n - 1 - j] for j in range(half)]
    out = [None] * n
    for a in range(half):
        even, odd = split(matrix, a)
        p, q = weigh(even, es), weigh(odd, os)
        out[a], out[n - 1 - a] = p + q, p - q
    return out


def kernel(
    load_hbm, stiff, bulk, shift, contact_hbm, tie, tab_hbm,
    sol, res,
    load, contact, tab, in_sem,
    X, V, EO, B0, FD, FM, RB, G,
    X1, B1, ID1,
    CO, PM, PG, HB, BP, R, D, T, INV, CE,
    load_next, contact_next,
    f_up, f_dn, f_from_prev, f_from_next,
    m_up, m_dn, m_from_prev, m_from_next,
    send, recv,
):
    p8, p4 = PLAN[NODES], PLAN[MID_NODES]
    w8, w4 = p8["w"], p4["w"]
    g = lax.axis_index("group")
    m = lax.axis_index("member")
    loops, members = lax.axis_size("group"), lax.axis_size("member")
    nxt, prv = lax.rem(m + 1, members), lax.rem(m + members - 1, members)
    slot = [0]
    pending = []

    def to_member(src, dst, target):
        i = slot[0]
        slot[0] += 1
        copy = pltpu.make_async_remote_copy(
            src_ref=src, dst_ref=dst, send_sem=send.at[i], recv_sem=recv.at[i],
            device_id={"member": target}, device_id_type=MESH,
        )
        copy.start()
        pending.append(copy)
        return copy

    def to_group(src, dst, offset):
        i = slot[0]
        slot[0] += 1
        copy = pltpu.make_async_remote_copy(
            src_ref=src, dst_ref=dst, send_sem=send.at[i], recv_sem=recv.at[i],
            device_id={"group": lax.rem(g + offset, loops)}, device_id_type=MESH,
        )
        copy.start()
        pending.append(copy)
        return copy

    def near(offset):
        return lax.rem(m + offset + members, members)

    reach = [o for d in range(1, REACH + 1) for o in (d, -d)]
    barrier = pltpu.get_barrier_semaphore()
    for offset in reach:
        pl.semaphore_signal(
            barrier, inc=1, device_id={"member": near(offset)}, device_id_type=MESH
        )
    for offset in range(1, loops):
        pl.semaphore_signal(
            barrier, inc=1, device_id={"group": lax.rem(g + offset, loops)}, device_id_type=MESH
        )
    inputs = [
        pltpu.make_async_copy(src, dst, in_sem.at[i])
        for i, (src, dst) in enumerate(
            ((tab_hbm, tab), (contact_hbm, contact), (load_hbm, load))
        )
    ]
    for copy in inputs:
        copy.start()
    pack = PM.at[REACH]
    pack[...] = jnp.concatenate(
        [stiff[...], bulk[...], shift[...], tie[...], jnp.zeros((2, LANES), jnp.float32)], axis=0
    )
    pl.semaphore_wait(barrier, len(reach) + loops - 1)

    setup = [
        to_member(PM.at[REACH], PM.at[REACH - 1], nxt),
        to_member(PM.at[REACH], PM.at[REACH + 1], prv),
        to_member(contact_hbm.at[0], contact_next, prv),
        to_member(load_hbm.at[:, 0], load_next, prv),
    ]
    packs = [
        to_member(PM.at[REACH], PM.at[REACH - o], near(o)) for o in reach if abs(o) > 1
    ]
    pack_prev, pack_next = PM.at[REACH - 1], PM.at[REACH + 1]
    for copy in inputs[:2]:
        copy.wait()

    def row(ref, i):
        return jnp.broadcast_to(ref[i : i + 1, :], (SUB, LANES))

    def quantities(ref):
        scale = 1.0 + row(ref, 3) * (1.0 / 3.0)
        return [scale * row(ref, 0), scale * row(ref, 1), scale * row(ref, 2), row(ref, 4)]

    third = row(pack, 3) * (1.0 / 3.0)
    CO[0] = third
    for base, plan in ((1, p8), (5, p4)):
        wk = tab[plan["wk"]]
        CO[base] = row(pack, 4) * wk
        for d in range(3):
            CO[base + 1 + d] = row(pack, d) * wk

    own_q = quantities(pack)

    def diagonal(plan, q, a, b):
        w, gg = plan["w"], plan["g"]
        wk, gk = tab[plan["wk"]], tab[plan["gk"]]
        inner = q[0] * float(gg[a] * w[b]) + q[1] * float(w[a] * gg[b]) + q[3] * float(w[a] * w[b])
        return inner * wk + q[2] * gk * float(w[a] * w[b])

    def edge(q):
        return [x + lane_up(x) for x in q]

    def fine_masks(a, ref, q):
        qe = edge(q)
        for b in range(NODES - 1):
            low = jnp.broadcast_to(ref[b, 0:1, :].astype(jnp.float32), (SUB, LANES))
            high = jnp.broadcast_to(ref[b, 1:2, :].astype(jnp.float32), (SUB, LANES))
            free = 1.0 - low * tab[PLAN["first"]] - high * tab[PLAN["last"]]
            FM[a, b] = free
            FD[a, b] = OMEGA * free / diagonal(p8, qe if b == 0 else q, a, b)

    def start_x(c, a, values):
        rhs = FM[a] * values
        B0[c, a] = rhs
        x = FD[a] * rhs
        X[c, a, 0 : NODES - 1] = x
        X[c, a, NODES - 1] = lane_down(x[0])

    for a in range(1, NODES - 1):
        fine_masks(a, contact.at[a], own_q)

    inputs[2].wait()

    @pl.loop(0, 3)
    def _(c):
        for a in range(1, NODES - 1):
            start_x(c, a, load[c, a])

    for copy in setup[:3]:
        copy.wait_recv()
    prev_q = [x + y for x, y in zip(own_q, quantities(pack_prev))]
    next_q = [x + y for x, y in zip(own_q, quantities(pack_next))]
    fine_masks(0, contact.at[0], prev_q)
    fine_masks(NODES - 1, contact_next, next_q)
    setup[3].wait_recv()

    @pl.loop(0, 3)
    def _(c):
        start_x(c, 0, load[c, 0])
        start_x(c, NODES - 1, load_next[c])

    last8 = NODES - 1

    def fine_prepare():
        for j in range(NODES // 2):
            k = last8 - j
            tj = CO[0] * (X[0, j] + X[1, j] + X[2, j])
            tk = CO[0] * (X[0, k] + X[1, k] + X[2, k])
            for c in range(3):
                vj, vk = X[c, j] + tj, X[c, k] + tk
                V[c, j], V[c, k] = vj, vk
                EO[c, j], EO[c, NODES // 2 + j] = vj + vk, vj - vk

    def fine_pair(c, a, planes=None):
        even, odd = split(p8["hat"], a)
        p = weigh(even, [EO[c, j] for j in range(NODES // 2)])
        q = weigh(odd, [EO[c, NODES // 2 + j] for j in range(NODES // 2)])
        out = []
        for plane, ya in ((a, p + q), (last8 - a, p - q)):
            v = V[c, plane]
            yk = sublanes(v, p8["along"], tab)
            base = CO[1] * X[c, plane] + CO[2] * ya + CO[4] * yk
            yb = centro(p8["hat"], [v[b] for b in range(NODES)])
            rows = [
                (base[b] + CO[3] * yb[b]) * float(w8[plane] * w8[b]) for b in range(NODES)
            ]
            rows[0] = rows[0] + lane_up(rows[last8])
            out.append(jnp.stack(rows[:last8], axis=0))
        return out

    def fine_update(c, a, z):
        x = X[c, a, 0:last8] + FD[a] * (B0[c, a] - z)
        X[c, a, 0:last8] = x
        X[c, a, last8] = lane_down(x[0])

    def fine_sweep(i, meanwhile=None):
        fine_prepare()

        @pl.loop(0, 3)
        def _(c):
            z = fine_pair(c, 0)
            f_dn[i, c], f_up[i, c] = z[0], z[1]

        up = to_member(f_up.at[i], f_from_prev.at[i], nxt)
        down = to_member(f_dn.at[i], f_from_next.at[i], prv)

        @pl.loop(0, 3)
        def _(c):
            for a in range(1, NODES // 2):
                z = fine_pair(c, a)
                fine_update(c, a, z[0])
                fine_update(c, last8 - a, z[1])

        if meanwhile is not None:
            meanwhile()
        up.wait_recv()
        down.wait_recv()

        @pl.loop(0, 3)
        def _(c):
            fine_update(c, 0, f_dn[i, c] + f_from_prev[i, c])
            fine_update(c, last8, f_up[i, c] + f_from_next[i, c])

    last4 = MID_NODES - 1
    coarse_data = {}

    def mid_setup():
        for copy in packs:
            copy.wait_recv()
        coarse_data["packs"] = [to_group(PM, PG.at[g], o) for o in range(1, loops)]
        pad = tab[PLAN["pad_mid"]]
        for a in range(MID_NODES):
            q = prev_q if a == 0 else next_q if a == last4 else own_q
            qe = edge(q)
            for b in range(last4):
                ID1[a, b] = OMEGA / (diagonal(p4, qe if b == 0 else q, a, b) + pad)

    low = tab[PLAN["low"]]

    def bundle(z):
        tiles = [z[c, b] for c in range(3) for b in range(last4)]
        rows = [tiles[2 * i] + pltpu.roll(tiles[2 * i + 1], 4, 0) for i in range(4)]
        return jnp.stack(rows + [tiles[8]], axis=0)

    def unbundle(rows):
        tiles = []
        for i in range(4):
            tiles.append(rows[i] * low)
            tiles.append(pltpu.roll(rows[i], 4, 0) * low)
        tiles.append(rows[4])
        return jnp.stack([jnp.stack(tiles[3 * c : 3 * c + 3], axis=0) for c in range(3)], axis=0)

    def mid_apply():
        us = [X1[a] for a in range(MID_NODES)]
        vs = [u + CO[0] * jnp.sum(u, axis=0, keepdims=True) for u in us]
        yas = centro(p4["hat"], vs)
        out = []
        for a in range(MID_NODES):
            yk = sublanes(vs[a], p4["along"], tab)
            base = CO[5] * us[a] + CO[6] * yas[a] + CO[8] * yk
            yb = centro(p4["hat"], [vs[a][:, b] for b in range(MID_NODES)])
            rows = [
                (base[:, b] + CO[7] * yb[b]) * float(w4[a] * w4[b]) for b in range(MID_NODES)
            ]
            rows[0] = rows[0] + lane_up(rows[last4])
            out.append(jnp.stack(rows[:last4], axis=1))
        return out

    def mid_store(a, x):
        X1[a, :, 0:last4] = x
        X1[a, :, last4] = lane_down(x[:, 0])

    mid_slot = [0]

    def mid_exchange(low_face, high_face):
        i = mid_slot[0]
        mid_slot[0] += 1
        m_dn[i], m_up[i] = bundle(low_face), bundle(high_face)
        up = to_member(m_up.at[i], m_from_prev.at[i], nxt)
        down = to_member(m_dn.at[i], m_from_next.at[i], prv)

        def arrive():
            up.wait_recv()
            down.wait_recv()
            return unbundle(m_from_prev[i]), unbundle(m_from_next[i])

        return arrive

    def mid_sweep():
        z = mid_apply()
        arrive = mid_exchange(z[0], z[last4])

        def update(a, total):
            mid_store(a, X1[a, :, 0:last4] + ID1[a] * (B1[a] - total))

        for a in range(1, last4):
            update(a, z[a])
        below, above = arrive()
        update(0, z[0] + below)
        update(last4, z[last4] + above)

    def wide_row(x):
        return jnp.broadcast_to(x, (SUB, LANES))

    def coarse_setup():
        for copy in coarse_data["packs"]:
            copy.wait_recv()
        PG[g] = PM[...]
        for i in range(PLANES):
            T[0, i] = jnp.zeros((SUB, LANES), jnp.float32)
        for s in range(2):
            for i in range(PLANES):
                D[s, 0, i] = jnp.zeros((SUB, LANES), jnp.float32)
                D[s, loops + 1, i] = jnp.zeros((SUB, LANES), jnp.float32)

        @pl.loop(0, loops)
        def _(h):
            alive = jnp.where(h < loops - 1, jnp.float32(1.0), jnp.float32(0.0))
            for i in range(PLANES):
                T[h + 1, i] = wide_row(PG[h, i + 1, 5:6, :] * alive)

        @pl.loop(0, loops)
        def _(h):
            parts = []
            for j in range(SPAN):
                s0, s1, s2 = (PG[h, j, d : d + 1, :] for d in range(3))
                b, t = PG[h, j, 3:4, :], PG[h, j, 4:5, :]
                parts.append((1.0 + b * (1.0 / 3.0)) * (s0 + s1 + s2) * 0.5 + t)
                if 1 <= j < SPAN - 1:
                    for k, x in enumerate((s0 * 0.5, s1 * 0.5, s2 * 0.5, t, b * (1.0 / 3.0))):
                        CE[k, h, j - 1] = wide_row(x)
            for i in range(PLANES):
                e = wide_row(parts[i] + parts[i + 1])
                INV[h, i] = 1.0 / (e + lane_up(e) + T[h + 1, i] + T[h, i])

    def coarse_step(s, h, first, second):
        now, later = s % 2, 1 - s % 2
        low, high = s, PLANES - 1 - s

        def derived(i):
            u = D[now, h + 1, i]
            total = sublanes(u, PLAN["csum"], tab)
            four = [
                u, u - sublanes(u, PLAN["kswap"], tab),
                total, total - sublanes(total, PLAN["kswap"], tab),
            ]
            return four, [lane_down(x) for x in four]

        carry = None
        left = derived(low)
        for e in range(low, high):
            right = derived(e + 1)
            h0, h1, h2, react, th = (CE[k, h, e] for k in range(5))
            v = [[x[0] + th * x[2] for x in side] for side in (left, right)]
            w = [[x[1] + th * x[3] for x in side] for side in (left, right)]
            u = [[x[0] for x in side] for side in (left, right)]
            da = [h0 * (v[0][b] - v[1][b]) for b in range(2)]
            db = [h1 * (v[a][0] - v[a][1]) for a in range(2)]
            sums = []
            for a in range(2):
                rows = []
                for b in range(2):
                    x = react * u[a][b] + h2 * w[a][b]
                    x = x + da[b] if a == 0 else x - da[b]
                    rows.append(x + db[a] if b == 0 else x - db[a])
                sums.append(rows[0] + lane_up(rows[1]))
            if carry is not None:
                d = D[now, h + 1, e]
                t, tu = T[h + 1, e], T[h, e]
                z = sums[0] + carry
                z = z + t * (d - D[now, h + 2, e]) + tu * (d - D[now, h, e])
                r = R[h, e] - z
                R[h, e] = r
                D[later, h + 1, e] = first * d + second * INV[h, e] * r
            carry = sums[1]
            left = right

    fine_sweep(0, mid_setup)

    jf, jc = PLAN["jf"], PLAN["jc"]
    fine_prepare()

    @pl.loop(0, 3)
    def _(c):
        for a in range(NODES // 2):
            z = fine_pair(c, a)
            for plane, value in ((a, z[0]), (last8 - a, z[1])):
                r = FM[plane] * value
                r = -r if plane == last8 else B0[c, plane] - r
                for bc in range(MID_NODES):
                    RB[plane, bc] = weigh(jf[:last8, bc], [r[b] for b in range(last8)])
        for plane in range(NODES):
            RB[plane, 0] = RB[plane, 0] + lane_up(RB[plane, last4])
        for ac in range(MID_NODES):
            part = weigh(jf[:, ac], [RB[a, 0:last4] for a in range(NODES)])
            G[ac, c] = sublanes(part, PLAN["jf_down"], tab)

    arrive = mid_exchange(G[0], G[last4])
    for a in range(1, last4):
        B1[a] = G[a]
        mid_store(a, ID1[a] * G[a])
    coarse_setup()
    below, above = arrive()
    for a, extra in ((0, below), (last4, above)):
        b1 = G[a] + extra
        B1[a] = b1
        mid_store(a, ID1[a] * b1)

    mid_sweep()
    z = mid_apply()
    rs = [B1[a] - z[a] for a in range(last4)] + [-z[last4]]
    hs = []
    for ac in range(2):
        part = weigh(jc[:, ac], rs)
        along = [weigh(jc[:last4, bc], [part[:, b] for b in range(last4)]) for bc in range(2)]
        along = along[0] + lane_up(along[1])
        total = None
        for c in range(3):
            term = sublanes(along[c], PLAN["jc_down"][c], tab)
            total = term if total is None else total + term
        hs.append(total)
    HB[REACH, 0], HB[REACH, 1] = hs[0], hs[1]
    halo = [to_member(HB.at[REACH], HB.at[REACH - o], near(o)) for o in reach]
    for copy in halo:
        copy.wait_recv()
    for i in range(PLANES):
        BP[i] = HB[i + 1, 0] + HB[i, 1]
    others = [to_group(BP, R.at[g], o) for o in range(1, loops)]
    R[g] = BP[...]
    center = 0.5 * (UPPER_BOUND + LOWER_BOUND)
    radius = 0.5 * (UPPER_BOUND - LOWER_BOUND)
    ratio = center / radius
    damping_now = 1.0 / ratio
    for copy in others:
        copy.wait_recv()

    @pl.loop(0, loops)
    def _(h):
        for i in range(PLANES):
            D[0, h + 1, i] = INV[h, i] * R[h, i] * (1.0 / center)

    x2 = [D[0, g + 1, REACH - 1], D[0, g + 1, REACH]]
    for s in range(CHEB - 1):
        damping_next = 1.0 / (2.0 * ratio - damping_now)
        first, second = damping_next * damping_now, 2.0 * damping_next / radius
        if s < CHEB - 2:
            @pl.loop(0, loops)
            def _(h):
                coarse_step(s, h, first, second)
        else:
            coarse_step(s, g, first, second)
        damping_now = damping_next
        x2 = [x + D[1 - s % 2, g + 1, REACH - 1 + a] for a, x in enumerate(x2)]

    wide = [[x, lane_down(x)] for x in x2]
    lifted = []
    for a in range(2):
        lifted.append(
            [
                jnp.stack([sublanes(wide[a][b], PLAN["jc_up"][c], tab) for c in range(3)], axis=0)
                for b in range(2)
            ]
        )
    for a in range(MID_NODES):
        cross = [weigh(jc[a], [lifted[0][b], lifted[1][b]]) for b in range(2)]
        add = jnp.stack([weigh(jc[b], cross) for b in range(last4)], axis=1)
        mid_store(a, X1[a, :, 0:last4] + add)
    mid_sweep()
    mid_sweep()

    @pl.loop(0, 3)
    def _(c):
        for a in range(MID_NODES):
            RB[a] = sublanes(X1[a, c], PLAN["jf_up"], tab)
        for a in range(NODES):
            part = weigh(jf[a], [RB[i] for i in range(MID_NODES)])
            add = jnp.stack(
                [weigh(jf[b], [part[i] for i in range(MID_NODES)]) for b in range(last8)], axis=0
            )
            x = X[c, a, 0:last8] + FM[a] * add
            X[c, a, 0:last8] = x
            X[c, a, last8] = lane_down(x[0])

    fine_sweep(1)
    fine_sweep(2)

    fine_prepare()

    @pl.loop(0, 3)
    def _(c):
        z = fine_pair(c, 0)
        f_dn[3, c], f_up[3, c] = z[0], z[1]

    final = to_member(f_up.at[3], f_from_prev.at[3], nxt)

    @pl.loop(0, 3)
    def _(c):
        for a in range(1, NODES // 2):
            z = fine_pair(c, a)
            res[c, a] = B0[c, a] - FM[a] * z[0]
            res[c, last8 - a] = B0[c, last8 - a] - FM[last8 - a] * z[1]
        for a in range(last8):
            sol[c, a] = X[c, a, 0:last8]

    final.wait_recv()

    @pl.loop(0, 3)
    def _(c):
        res[c, 0] = B0[c, 0] - FM[0] * (f_dn[3, c] + f_from_prev[3, c])

    for copy in pending:
        copy.wait_send()


def body(load, stiffness_dir, bulk_ratio, thermal_shift, contact, loop_tie):
    f32 = jnp.float32
    n, q, o = NODES, MID_NODES, NODES - 1
    tile = (SUB, LANES)

    def vmem(*shape):
        return pltpu.VMEM(shape, f32)

    spec = pl.BlockSpec(memory_space=pltpu.VMEM)
    slots = 60
    loops = lax.axis_size("group")
    hbm = pl.BlockSpec(memory_space=pltpu.HBM)
    scratch = [
        vmem(3, o, o, *tile), pltpu.VMEM((o, o, 2, LANES), jnp.int32), vmem(*TABLE.shape),
        pltpu.SemaphoreType.DMA((3,)),
        vmem(3, n, n, *tile), vmem(3, n, n, *tile), vmem(3, n, n, *tile),
        vmem(3, n, o, *tile), vmem(n, o, *tile), vmem(n, o, *tile),
        vmem(n, q, *tile), vmem(q, 3, q - 1, *tile),
        vmem(q, 3, q, *tile), vmem(q, 3, q - 1, *tile), vmem(q, q - 1, *tile),
        vmem(9, *tile),
        vmem(SPAN, *tile), vmem(loops, SPAN, *tile), vmem(SPAN, 2, *tile),
        vmem(PLANES, *tile), vmem(loops, PLANES, *tile),
        vmem(2, loops + 2, PLANES, *tile), vmem(loops + 1, PLANES, *tile),
        vmem(loops, PLANES, *tile), vmem(5, loops, PLANES - 1, *tile),
        vmem(3, o, *tile), pltpu.VMEM((o, 2, LANES), jnp.int32),
    ]
    scratch += [vmem(4, 3, o, *tile) for _ in range(4)]
    scratch += [vmem(4, 5, *tile) for _ in range(4)]
    scratch += [
        pltpu.SemaphoreType.DMA((slots,)),
        pltpu.SemaphoreType.DMA((slots,)),
    ]
    shape = jax.ShapeDtypeStruct(load.shape, f32)
    return pl.pallas_call(
        kernel,
        out_shape=(shape, shape),
        in_specs=[hbm, spec, spec, spec, hbm, spec, hbm],
        out_specs=(spec, spec),
        scratch_shapes=scratch,
        compiler_params=pltpu.CompilerParams(
            collective_id=0, has_side_effects=True, vmem_limit_bytes=48 * 2**20
        ),
    )(
        load,
        stiffness_dir,
        bulk_ratio.reshape(1, LANES),
        thermal_shift.reshape(1, LANES),
        contact.transpose(1, 2, 0, 3),
        loop_tie.reshape(1, LANES),
        jnp.asarray(TABLE),
    )


def solution(mesh):
    in_specs = (
        P(None, None, None, None, ("group", "member")),
        P(None, ("group", "member")),
        P(("group", "member")),
        P(("group", "member")),
        P(None, None, None, ("group", "member")),
        P(("group", "member")),
    )
    out_specs = (
        P(None, None, None, None, ("group", "member")),
        P(None, None, None, None, ("group", "member")),
    )
    return jax.shard_map(body, mesh=mesh, in_specs=in_specs, out_specs=out_specs, check_vma=False)
```

```python
import functools

import jax
import jax.numpy as jnp
import numpy as np
from jax import lax
from jax.experimental import pallas as pl
from jax.experimental.pallas import tpu as pltpu
from jax.sharding import PartitionSpec as P

NODES = 8
MID_NODES = 4
COARSE_NODES = 2
SWEEPS = 2
CHEB = 6

OMEGA = 0.3
LOWER_BOUND = 0.3
UPPER_BOUND = 3.0
MESH = pl.DeviceIdType.MESH
REACH = CHEB
SPAN = 2 * REACH + 1
PLANES = 2 * REACH
LANES = 128
SUB = 8


def tables(resolution):
    indices = np.arange(resolution)
    points = -np.cos(np.pi * indices / (resolution - 1))
    padded = np.concatenate([points[:1], points, points[-1:]])
    weights = (padded[2:] - padded[:-2]) / 2.0
    factor = np.where((indices == 0) | (indices == resolution - 1), 2.0, 1.0)
    spacing = points[:, None] - points[None, :] + np.eye(resolution)
    parity = np.where((indices[:, None] + indices[None, :]) % 2 == 0, 1.0, -1.0)
    offdiag = (1.0 - np.eye(resolution)) * factor[:, None] / factor[None, :] * parity / spacing
    derivative = offdiag - np.eye(resolution) * offdiag.sum(axis=1)[:, None]
    stiffness = (weights[:, None] * derivative * derivative).sum(axis=0)
    return (points, weights, derivative, stiffness)


def interpolation(fine_count, coarse_count):
    fine_points = tables(fine_count)[0]
    coarse_points = tables(coarse_count)[0]
    columns = []
    for column in range(coarse_count):
        values = np.ones(fine_count)
        for partner in range(coarse_count):
            if partner != column:
                values = (
                    values
                    * (fine_points - coarse_points[partner])
                    / (coarse_points[column] - coarse_points[partner])
                )
        columns.append(values)
    return np.stack(columns, axis=1)


class Columns:
    def __init__(self):
        self.rows, self.index = [], {}

    def add(self, column):
        column = np.asarray(column, np.float32)
        key = tuple(column.tolist())
        if key not in self.index:
            self.index[key] = len(self.rows)
            self.rows.append(column)
        return self.index[key]

    def matrix(self, values):
        full = np.zeros((SUB, SUB))
        full[: values.shape[0], : values.shape[1]] = values
        terms = []
        for shift in range(SUB):
            column = [full[s, (s - shift) % SUB] for s in range(SUB)]
            if np.any(column):
                terms.append((shift, self.add(column)))
        return terms

    def table(self):
        return np.repeat(np.stack(self.rows)[:, :, None], LANES, axis=2)


def padded(values):
    return np.concatenate([values, np.zeros(SUB - len(values))])


def make_plan():
    cols = Columns()
    plan = {}
    for n in (NODES, MID_NODES):
        _, w, d, g = tables(n)
        hat = (d.T @ np.diag(w) @ d) / w[:, None]
        plan[n] = dict(
            n=n, w=w, g=g, hat=hat, along=cols.matrix(hat), wk=cols.add(padded(w)), gk=cols.add(padded(g)),
        )
    pad = np.ones(SUB)
    pad[:MID_NODES] = 0.0
    plan["pad_mid"] = cols.add(pad)
    first, last = np.zeros(SUB), np.zeros(SUB)
    first[0], last[SUB - 1] = 1.0, 1.0
    plan["first"], plan["last"] = cols.add(first), cols.add(last)
    jf = interpolation(NODES, MID_NODES)
    jc = interpolation(MID_NODES, COARSE_NODES)
    plan["jf"], plan["jc"] = jf, jc
    plan["jf_up"], plan["jf_down"] = cols.matrix(jf), cols.matrix(jf.T)
    low = np.zeros(SUB)
    low[:MID_NODES] = 1.0
    plan["low"] = cols.add(low)
    down, up = [], []
    for c in range(3):
        m = np.zeros((SUB, SUB))
        m[2 * c : 2 * c + 2, :MID_NODES] = jc.T
        down.append(cols.matrix(m))
        m = np.zeros((SUB, SUB))
        m[:MID_NODES, 2 * c : 2 * c + 2] = jc
        up.append(cols.matrix(m))
    plan["jc_down"], plan["jc_up"] = down, up
    m = np.zeros((SUB, SUB))
    swap = np.zeros((SUB, SUB))
    for c in range(3):
        for k in range(2):
            swap[2 * c + k, 2 * c + 1 - k] = 1.0
            for e in range(3):
                m[2 * c + k, 2 * e + k] = 1.0
    eye = np.diag(np.where(np.arange(SUB) < 6, 1.0, 0.0))
    plan["derived"] = [cols.matrix(x) for x in (eye - swap, m, m - swap @ m)]
    return plan, cols.table()


PLAN, TABLE = make_plan()


def lane_up(x):
    return pltpu.roll(x, 1, x.ndim - 1)


def lane_down(x):
    return pltpu.roll(x, LANES - 1, x.ndim - 1)


def weigh(scalars, arrays):
    total = None
    for s, x in zip(scalars, arrays):
        s = float(s)
        if s == 0.0:
            continue
        term = x if s == 1.0 else x * s
        total = term if total is None else total + term
    return total


def sublanes(x, terms, tab):
    total = None
    for shift, column in terms:
        moved = x if shift == 0 else pltpu.roll(x, shift, x.ndim - 2)
        term = moved * tab[column]
        total = term if total is None else total + term
    return total


def tree(terms):
    while len(terms) > 1:
        pairs = [terms[i] + terms[i + 1] for i in range(0, len(terms) - 1, 2)]
        terms = pairs + terms[2 * len(pairs) :]
    return terms[0]


def split(matrix, a):
    n = matrix.shape[0]
    half = n // 2
    even = [(matrix[a, j] + matrix[a, n - 1 - j]) / 2 for j in range(half)]
    odd = [(matrix[a, j] - matrix[a, n - 1 - j]) / 2 for j in range(half)]
    return even, odd


def centro(matrix, xs):
    n = matrix.shape[0]
    half = n // 2
    es = [xs[j] + xs[n - 1 - j] for j in range(half)]
    os = [xs[j] - xs[n - 1 - j] for j in range(half)]
    out = [None] * n
    for a in range(half):
        even, odd = split(matrix, a)
        p, q = weigh(even, es), weigh(odd, os)
        out[a], out[n - 1 - a] = p + q, p - q
    return out


def kernel(
    load_hbm, stiff_hbm, bulk_hbm, shift_hbm, contact_hbm, tie_hbm, tab_hbm,
    sol, res,
    load, contact, tab, stiff, bulk, shift, tie, in_sem,
    X, V, EO, B0, FD, FM, RB, G,
    X1, B1, ID1,
    CO, PM, PG, HB, BP, R, D, T, INV, CE,
    load_next, contact_next,
    f_up, f_dn, f_from_prev, f_from_next,
    m_up, m_dn, m_from_prev, m_from_next,
    send, recv,
):
    p8, p4 = PLAN[NODES], PLAN[MID_NODES]
    w8, w4 = p8["w"], p4["w"]
    g = lax.axis_index("group")
    m = lax.axis_index("member")
    loops, members = lax.axis_size("group"), lax.axis_size("member")
    nxt, prv = lax.rem(m + 1, members), lax.rem(m + members - 1, members)
    slot = [0]
    pending = []

    def to_member(src, dst, target):
        i = slot[0]
        slot[0] += 1
        copy = pltpu.make_async_remote_copy(
            src_ref=src, dst_ref=dst, send_sem=send.at[i], recv_sem=recv.at[i],
            device_id={"member": target}, device_id_type=MESH,
        )
        copy.start()
        pending.append(copy)
        return copy

    def to_group(src, dst, offset):
        i = slot[0]
        slot[0] += 1
        copy = pltpu.make_async_remote_copy(
            src_ref=src, dst_ref=dst, send_sem=send.at[i], recv_sem=recv.at[i],
            device_id={"group": lax.rem(g + offset, loops)}, device_id_type=MESH,
        )
        copy.start()
        pending.append(copy)
        return copy

    def near(offset):
        return lax.rem(m + offset + members, members)

    reach = [o for d in range(1, REACH + 1) for o in (d, -d)]
    barrier = pltpu.get_barrier_semaphore()
    for offset in reach:
        pl.semaphore_signal(
            barrier, inc=1, device_id={"member": near(offset)}, device_id_type=MESH
        )
    for offset in range(1, loops):
        pl.semaphore_signal(
            barrier, inc=1, device_id={"group": lax.rem(g + offset, loops)}, device_id_type=MESH
        )
    inputs = [
        pltpu.make_async_copy(src, dst, in_sem.at[i])
        for i, (src, dst) in enumerate(
            (
                (stiff_hbm, stiff), (bulk_hbm, bulk), (shift_hbm, shift), (tie_hbm, tie),
                (tab_hbm, tab), (contact_hbm, contact), (load_hbm, load),
            )
        )
    ]
    for copy in inputs:
        copy.start()
    for copy in inputs[:4]:
        copy.wait()
    pack = PM.at[REACH]
    pack[...] = jnp.concatenate(
        [stiff[...], bulk[...], shift[...], tie[...], jnp.zeros((2, LANES), jnp.float32)], axis=0
    )
    pl.semaphore_wait(barrier, len(reach) + loops - 1)

    setup = [
        to_member(PM.at[REACH], PM.at[REACH - 1], nxt),
        to_member(PM.at[REACH], PM.at[REACH + 1], prv),
        to_member(contact_hbm.at[0], contact_next, prv),
        to_member(load_hbm.at[:, 0], load_next, prv),
    ]
    packs = [
        to_member(PM.at[REACH], PM.at[REACH - o], near(o)) for o in reach if abs(o) > 1
    ]
    pack_prev, pack_next = PM.at[REACH - 1], PM.at[REACH + 1]
    for copy in inputs[4:6]:
        copy.wait()

    def row(ref, i):
        return jnp.broadcast_to(ref[i : i + 1, :], (SUB, LANES))

    def quantities(ref):
        scale = 1.0 + row(ref, 3) * (1.0 / 3.0)
        return [scale * row(ref, 0), scale * row(ref, 1), scale * row(ref, 2), row(ref, 4)]

    third = row(pack, 3) * (1.0 / 3.0)
    CO[0] = third
    for base, plan in ((1, p8), (5, p4)):
        wk = tab[plan["wk"]]
        CO[base] = row(pack, 4) * wk
        for d in range(3):
            CO[base + 1 + d] = row(pack, d) * wk

    own_q = quantities(pack)

    def diagonal(plan, q, a, b):
        w, gg = plan["w"], plan["g"]
        wk, gk = tab[plan["wk"]], tab[plan["gk"]]
        inner = q[0] * float(gg[a] * w[b]) + q[1] * float(w[a] * gg[b]) + q[3] * float(w[a] * w[b])
        return inner * wk + q[2] * gk * float(w[a] * w[b])

    def edge(q):
        return [x + lane_up(x) for x in q]

    def fine_masks(a, ref, q):
        qe = edge(q)
        for b in range(NODES - 1):
            low = jnp.broadcast_to(ref[b, 0:1, :].astype(jnp.float32), (SUB, LANES))
            high = jnp.broadcast_to(ref[b, 1:2, :].astype(jnp.float32), (SUB, LANES))
            free = 1.0 - low * tab[PLAN["first"]] - high * tab[PLAN["last"]]
            FM[a, b] = free
            FD[a, b] = OMEGA * free / diagonal(p8, qe if b == 0 else q, a, b)

    def start_x(c, a, values):
        rhs = FM[a] * values
        B0[c, a] = rhs
        x = FD[a] * rhs
        X[c, a, 0 : NODES - 1] = x
        X[c, a, NODES - 1] = lane_down(x[0])

    for a in range(1, NODES - 1):
        fine_masks(a, contact.at[a], own_q)

    inputs[6].wait()

    @pl.loop(0, 3)
    def _(c):
        for a in range(1, NODES - 1):
            start_x(c, a, load[c, a])

    for copy in setup[:3]:
        copy.wait_recv()
    prev_q = [x + y for x, y in zip(own_q, quantities(pack_prev))]
    next_q = [x + y for x, y in zip(own_q, quantities(pack_next))]
    fine_masks(0, contact.at[0], prev_q)
    fine_masks(NODES - 1, contact_next, next_q)
    setup[3].wait_recv()

    @pl.loop(0, 3)
    def _(c):
        start_x(c, 0, load[c, 0])
        start_x(c, NODES - 1, load_next[c])

    last8 = NODES - 1

    inner = range(1, NODES // 2)

    def fine_prepare(pairs):
        for j in pairs:
            k = last8 - j
            tj = CO[0] * (X[0, j] + X[1, j] + X[2, j])
            tk = CO[0] * (X[0, k] + X[1, k] + X[2, k])
            for c in range(3):
                vj, vk = X[c, j] + tj, X[c, k] + tk
                V[c, j], V[c, k] = vj, vk
                EO[c, j], EO[c, NODES // 2 + j] = vj + vk, vj - vk

    def fine_pair(c, a, planes=None):
        even, odd = split(p8["hat"], a)
        p = weigh(even, [EO[c, j] for j in range(NODES // 2)])
        q = weigh(odd, [EO[c, NODES // 2 + j] for j in range(NODES // 2)])
        out = []
        for plane, ya in ((a, p + q), (last8 - a, p - q)):
            v = V[c, plane]
            yk = sublanes(v, p8["along"], tab)
            base = CO[1] * X[c, plane] + CO[2] * ya + CO[4] * yk
            yb = centro(p8["hat"], [v[b] for b in range(NODES)])
            rows = [
                (base[b] + CO[3] * yb[b]) * float(w8[plane] * w8[b]) for b in range(NODES)
            ]
            rows[0] = rows[0] + lane_up(rows[last8])
            out.append(jnp.stack(rows[:last8], axis=0))
        return out

    def fine_update(c, a, z):
        x = X[c, a, 0:last8] + FD[a] * (B0[c, a] - z)
        X[c, a, 0:last8] = x
        X[c, a, last8] = lane_down(x[0])

    def fine_faces(i, both=True):
        copies = []
        for c in range(3):
            z = fine_pair(c, 0)
            f_dn[i, c], f_up[i, c] = z[0], z[1]
            copies.append([to_member(f_up.at[i, c], f_from_prev.at[i, c], nxt)])
            if both:
                copies[c].append(to_member(f_dn.at[i, c], f_from_next.at[i, c], prv))
        return copies

    def fine_sweep(i, meanwhile=None):
        fine_prepare([0])
        copies = fine_faces(i)

        @pl.loop(0, 3)
        def _(c):
            for a in inner:
                z = fine_pair(c, a)
                fine_update(c, a, z[0])
                fine_update(c, last8 - a, z[1])

        fine_prepare(inner)
        if meanwhile is not None:
            meanwhile()
        for c in range(3):
            for copy in copies[c]:
                copy.wait_recv()
            fine_update(c, 0, f_dn[i, c] + f_from_prev[i, c])
            fine_update(c, last8, f_up[i, c] + f_from_next[i, c])

    last4 = MID_NODES - 1
    coarse_data = {}

    def mid_setup():
        for copy in packs:
            copy.wait_recv()
        coarse_data["packs"] = [to_group(PM, PG.at[g], o) for o in range(1, loops)]
        pad = tab[PLAN["pad_mid"]]
        for a in range(MID_NODES):
            q = prev_q if a == 0 else next_q if a == last4 else own_q
            qe = edge(q)
            for b in range(last4):
                ID1[a, b] = OMEGA / (diagonal(p4, qe if b == 0 else q, a, b) + pad)

    low = tab[PLAN["low"]]

    def bundle(z):
        tiles = [z[c, b] for c in range(3) for b in range(last4)]
        rows = [tiles[2 * i] + pltpu.roll(tiles[2 * i + 1], 4, 0) for i in range(4)]
        return jnp.stack(rows + [tiles[8]], axis=0)

    def unbundle(rows):
        tiles = []
        for i in range(4):
            tiles.append(rows[i] * low)
            tiles.append(pltpu.roll(rows[i], 4, 0) * low)
        tiles.append(rows[4])
        return jnp.stack([jnp.stack(tiles[3 * c : 3 * c + 3], axis=0) for c in range(3)], axis=0)

    def mid_apply():
        us = [X1[a] for a in range(MID_NODES)]
        vs = [u + CO[0] * jnp.sum(u, axis=0, keepdims=True) for u in us]
        half = MID_NODES // 2
        es = [vs[j] + vs[last4 - j] for j in range(half)]
        os = [vs[j] - vs[last4 - j] for j in range(half)]

        def pair(a):
            even, odd = split(p4["hat"], a)
            p, q = weigh(even, es), weigh(odd, os)
            out = []
            for plane, ya in ((a, p + q), (last4 - a, p - q)):
                yk = sublanes(vs[plane], p4["along"], tab)
                base = CO[5] * us[plane] + CO[6] * ya + CO[8] * yk
                yb = centro(p4["hat"], [vs[plane][:, b] for b in range(MID_NODES)])
                rows = [
                    (base[:, b] + CO[7] * yb[b]) * float(w4[plane] * w4[b])
                    for b in range(MID_NODES)
                ]
                rows[0] = rows[0] + lane_up(rows[last4])
                out.append(jnp.stack(rows[:last4], axis=1))
            return out

        return pair

    def mid_store(a, x):
        X1[a, :, 0:last4] = x
        X1[a, :, last4] = lane_down(x[:, 0])

    mid_slot = [0]

    def mid_exchange(low_face, high_face):
        i = mid_slot[0]
        mid_slot[0] += 1
        m_dn[i], m_up[i] = bundle(low_face), bundle(high_face)
        up = to_member(m_up.at[i], m_from_prev.at[i], nxt)
        down = to_member(m_dn.at[i], m_from_next.at[i], prv)

        def arrive():
            up.wait_recv()
            down.wait_recv()
            return unbundle(m_from_prev[i]), unbundle(m_from_next[i])

        return arrive

    def mid_sweep():
        pair = mid_apply()
        faces = pair(0)
        arrive = mid_exchange(faces[0], faces[1])
        z = [faces[0], *pair(1), faces[1]]

        def update(a, total):
            mid_store(a, X1[a, :, 0:last4] + ID1[a] * (B1[a] - total))

        for a in range(1, last4):
            update(a, z[a])
        below, above = arrive()
        update(0, z[0] + below)
        update(last4, z[last4] + above)

    def wide_row(x):
        return jnp.broadcast_to(x, (SUB, LANES))

    def coarse_setup():
        for copy in coarse_data["packs"]:
            copy.wait_recv()
        PG[g] = PM[...]
        for i in range(PLANES):
            T[0, i] = jnp.zeros((SUB, LANES), jnp.float32)
        for s in range(2):
            for i in range(PLANES):
                D[s, 0, i] = jnp.zeros((SUB, LANES), jnp.float32)
                D[s, loops + 1, i] = jnp.zeros((SUB, LANES), jnp.float32)

        @pl.loop(0, loops)
        def _(h):
            alive = jnp.where(h < loops - 1, jnp.float32(1.0), jnp.float32(0.0))
            for i in range(PLANES):
                T[h + 1, i] = wide_row(PG[h, i + 1, 5:6, :] * alive)

        @pl.loop(0, loops)
        def _(h):
            parts = []
            for j in range(SPAN):
                s0, s1, s2 = (PG[h, j, d : d + 1, :] for d in range(3))
                b, t = PG[h, j, 3:4, :], PG[h, j, 4:5, :]
                parts.append((1.0 + b * (1.0 / 3.0)) * (s0 + s1 + s2) * 0.5 + t)
                if 1 <= j < SPAN - 1:
                    for k, x in enumerate((s0 * 0.5, s1 * 0.5, s2 * 0.5, t, b * (1.0 / 3.0))):
                        CE[k, h, j - 1] = wide_row(x)
            for i in range(PLANES):
                e = wide_row(parts[i] + parts[i + 1])
                INV[h, i] = 1.0 / (e + lane_up(e) + T[h + 1, i] + T[h, i])

    def coarse_step(s, h, first, second):
        now, later = s % 2, 1 - s % 2
        low, high = s, PLANES - 1 - s

        def derived(i):
            u = D[now, h + 1, i]
            rolled = [u] + [pltpu.roll(u, r, 0) for r in range(1, SUB)]
            four = [u]
            for terms in PLAN["derived"]:
                four.append(tree([rolled[r] * tab[column] for r, column in terms]))
            return four, [lane_down(x) for x in four]

        carry = None
        left = derived(low)
        for e in range(low, high):
            right = derived(e + 1)
            h0, h1, h2, react, th = (CE[k, h, e] for k in range(5))
            v = [[x[0] + th * x[2] for x in side] for side in (left, right)]
            w = [[x[1] + th * x[3] for x in side] for side in (left, right)]
            u = [[x[0] for x in side] for side in (left, right)]
            da = [h0 * (v[0][b] - v[1][b]) for b in range(2)]
            db = [h1 * (v[a][0] - v[a][1]) for a in range(2)]
            sums = []
            for a in range(2):
                rows = []
                for b in range(2):
                    x = react * u[a][b] + h2 * w[a][b]
                    x = x + da[b] if a == 0 else x - da[b]
                    rows.append(x + db[a] if b == 0 else x - db[a])
                sums.append(rows[0] + lane_up(rows[1]))
            if carry is not None:
                d = D[now, h + 1, e]
                t, tu = T[h + 1, e], T[h, e]
                z = sums[0] + carry
                z = z + t * (d - D[now, h + 2, e]) + tu * (d - D[now, h, e])
                r = R[h, e] - z
                R[h, e] = r
                D[later, h + 1, e] = first * d + second * INV[h, e] * r
            carry = sums[1]
            left = right

    fine_prepare(inner)
    fine_sweep(0, mid_setup)

    jf, jc = PLAN["jf"], PLAN["jc"]
    fine_prepare([0])

    @pl.loop(0, 3)
    def _(c):
        for a in range(NODES // 2):
            z = fine_pair(c, a)
            for plane, value in ((a, z[0]), (last8 - a, z[1])):
                r = FM[plane] * value
                r = -r if plane == last8 else B0[c, plane] - r
                for bc in range(MID_NODES):
                    RB[plane, bc] = weigh(jf[:last8, bc], [r[b] for b in range(last8)])
        for plane in range(NODES):
            RB[plane, 0] = RB[plane, 0] + lane_up(RB[plane, last4])
        for ac in range(MID_NODES):
            part = weigh(jf[:, ac], [RB[a, 0:last4] for a in range(NODES)])
            G[ac, c] = sublanes(part, PLAN["jf_down"], tab)

    arrive = mid_exchange(G[0], G[last4])
    for a in range(1, last4):
        B1[a] = G[a]
        mid_store(a, ID1[a] * G[a])
    coarse_setup()
    below, above = arrive()
    for a, extra in ((0, below), (last4, above)):
        b1 = G[a] + extra
        B1[a] = b1
        mid_store(a, ID1[a] * b1)

    mid_sweep()
    pair = mid_apply()
    faces = pair(0)
    z = [faces[0], *pair(1), faces[1]]
    rs = [B1[a] - z[a] for a in range(last4)] + [-z[last4]]
    hs = []
    for ac in range(2):
        part = weigh(jc[:, ac], rs)
        along = [weigh(jc[:last4, bc], [part[:, b] for b in range(last4)]) for bc in range(2)]
        along = along[0] + lane_up(along[1])
        total = None
        for c in range(3):
            term = sublanes(along[c], PLAN["jc_down"][c], tab)
            total = term if total is None else total + term
        hs.append(total)
    HB[REACH, 0], HB[REACH, 1] = hs[0], hs[1]
    halo = [to_member(HB.at[REACH], HB.at[REACH - o], near(o)) for o in reach]
    inside = REACH // 2
    for copy in halo[: 2 * inside]:
        copy.wait_recv()
    mid_low, mid_high = inside, PLANES - inside
    others = []

    def planes_out(low, high):
        for o in range(1, loops):
            cut = min(o, loops - o)
            first, last = max(low, cut), min(high, PLANES - cut)
            if first < last:
                part = pl.ds(first, last - first)
                others.append(to_group(BP.at[part], R.at[g, part], o))

    for i in range(mid_low, mid_high):
        BP[i] = HB[i + 1, 0] + HB[i, 1]
    planes_out(mid_low, mid_high)
    for copy in halo[2 * inside :]:
        copy.wait_recv()
    for i in [*range(mid_low), *range(mid_high, PLANES)]:
        BP[i] = HB[i + 1, 0] + HB[i, 1]
    planes_out(0, mid_low)
    planes_out(mid_high, PLANES)
    R[g] = BP[...]
    center = 0.5 * (UPPER_BOUND + LOWER_BOUND)
    radius = 0.5 * (UPPER_BOUND - LOWER_BOUND)
    ratio = center / radius
    damping_now = 1.0 / ratio
    for copy in others:
        copy.wait_recv()

    @pl.loop(0, loops)
    def _(h):
        for i in range(PLANES):
            D[0, h + 1, i] = INV[h, i] * R[h, i] * (1.0 / center)

    x2 = [D[0, g + 1, REACH - 1], D[0, g + 1, REACH]]
    for s in range(CHEB - 1):
        damping_next = 1.0 / (2.0 * ratio - damping_now)
        first, second = damping_next * damping_now, 2.0 * damping_next / radius
        if s < CHEB - 2:
            for h in range(loops):
                coarse_step(s, h, first, second)
        else:
            coarse_step(s, g, first, second)
        damping_now = damping_next
        x2 = [x + D[1 - s % 2, g + 1, REACH - 1 + a] for a, x in enumerate(x2)]

    wide = [[x, lane_down(x)] for x in x2]
    lifted = []
    for a in range(2):
        lifted.append(
            [
                jnp.stack([sublanes(wide[a][b], PLAN["jc_up"][c], tab) for c in range(3)], axis=0)
                for b in range(2)
            ]
        )
    for a in range(MID_NODES):
        cross = [weigh(jc[a], [lifted[0][b], lifted[1][b]]) for b in range(2)]
        add = jnp.stack([weigh(jc[b], cross) for b in range(last4)], axis=1)
        mid_store(a, X1[a, :, 0:last4] + add)
    mid_sweep()
    mid_sweep()

    @pl.loop(0, 3)
    def _(c):
        for a in range(MID_NODES):
            RB[a] = sublanes(X1[a, c], PLAN["jf_up"], tab)
        for a in range(NODES):
            part = weigh(jf[a], [RB[i] for i in range(MID_NODES)])
            add = jnp.stack(
                [weigh(jf[b], [part[i] for i in range(MID_NODES)]) for b in range(last8)], axis=0
            )
            x = X[c, a, 0:last8] + FM[a] * add
            X[c, a, 0:last8] = x
            X[c, a, last8] = lane_down(x[0])

    fine_prepare(inner)
    fine_sweep(1)
    fine_sweep(2)

    fine_prepare([0])
    final = fine_faces(3, both=False)

    @pl.loop(0, 3)
    def _(c):
        for a in range(1, NODES // 2):
            z = fine_pair(c, a)
            res[c, a] = B0[c, a] - FM[a] * z[0]
            res[c, last8 - a] = B0[c, last8 - a] - FM[last8 - a] * z[1]
        for a in range(last8):
            sol[c, a] = X[c, a, 0:last8]

    for c in range(3):
        final[c][0].wait_recv()
        res[c, 0] = B0[c, 0] - FM[0] * (f_dn[3, c] + f_from_prev[3, c])

    for copy in pending:
        copy.wait_send()


def body(load, stiffness_dir, bulk_ratio, thermal_shift, contact, loop_tie):
    f32 = jnp.float32
    n, q, o = NODES, MID_NODES, NODES - 1
    tile = (SUB, LANES)

    def vmem(*shape):
        return pltpu.VMEM(shape, f32)

    spec = pl.BlockSpec(memory_space=pltpu.VMEM)
    slots = 80
    loops = lax.axis_size("group")
    hbm = pl.BlockSpec(memory_space=pltpu.HBM)
    scratch = [
        vmem(3, o, o, *tile), pltpu.VMEM((o, o, 2, LANES), jnp.int32), vmem(*TABLE.shape),
        vmem(3, LANES), vmem(1, LANES), vmem(1, LANES), vmem(1, LANES),
        pltpu.SemaphoreType.DMA((7,)),
        vmem(3, n, n, *tile), vmem(3, n, n, *tile), vmem(3, n, n, *tile),
        vmem(3, n, o, *tile), vmem(n, o, *tile), vmem(n, o, *tile),
        vmem(n, q, *tile), vmem(q, 3, q - 1, *tile),
        vmem(q, 3, q, *tile), vmem(q, 3, q - 1, *tile), vmem(q, q - 1, *tile),
        vmem(9, *tile),
        vmem(SPAN, *tile), vmem(loops, SPAN, *tile), vmem(SPAN, 2, *tile),
        vmem(PLANES, *tile), vmem(loops, PLANES, *tile),
        vmem(2, loops + 2, PLANES, *tile), vmem(loops + 1, PLANES, *tile),
        vmem(loops, PLANES, *tile), vmem(5, loops, PLANES - 1, *tile),
        vmem(3, o, *tile), pltpu.VMEM((o, 2, LANES), jnp.int32),
    ]
    scratch += [vmem(4, 3, o, *tile) for _ in range(4)]
    scratch += [vmem(4, 5, *tile) for _ in range(4)]
    scratch += [
        pltpu.SemaphoreType.DMA((slots,)),
        pltpu.SemaphoreType.DMA((slots,)),
    ]
    shape = jax.ShapeDtypeStruct(load.shape, f32)
    return pl.pallas_call(
        kernel,
        out_shape=(shape, shape),
        in_specs=[hbm] * 7,
        out_specs=(spec, spec),
        scratch_shapes=scratch,
        compiler_params=pltpu.CompilerParams(
            collective_id=0, has_side_effects=True, vmem_limit_bytes=48 * 2**20
        ),
    )(
        *(
            pltpu.with_memory_space_constraint(x, pltpu.HBM)
            for x in (
                load,
                stiffness_dir,
                bulk_ratio.reshape(1, LANES),
                thermal_shift.reshape(1, LANES),
                contact.transpose(1, 2, 0, 3),
                loop_tie.reshape(1, LANES),
                jnp.asarray(TABLE),
            )
        )
    )


def solution(mesh):
    in_specs = (
        P(None, None, None, None, ("group", "member")),
        P(None, ("group", "member")),
        P(("group", "member")),
        P(("group", "member")),
        P(None, None, None, ("group", "member")),
        P(("group", "member")),
    )
    out_specs = (
        P(None, None, None, None, ("group", "member")),
        P(None, None, None, None, ("group", "member")),
    )
    return jax.shard_map(body, mesh=mesh, in_specs=in_specs, out_specs=out_specs, check_vma=False)
```

```python
import functools

import jax
import jax.numpy as jnp
import numpy as np
from jax import lax
from jax.experimental import pallas as pl
from jax.experimental.pallas import tpu as pltpu
from jax.sharding import PartitionSpec as P

NODES = 8
MID_NODES = 4
COARSE_NODES = 2
SWEEPS = 2
CHEB = 6

OMEGA = 0.3
LOWER_BOUND = 0.3
UPPER_BOUND = 3.0
MESH = pl.DeviceIdType.MESH
REACH = CHEB
SPAN = 2 * REACH + 1
PLANES = 2 * REACH
LANES = 128
SUB = 8


def tables(resolution):
    indices = np.arange(resolution)
    points = -np.cos(np.pi * indices / (resolution - 1))
    padded = np.concatenate([points[:1], points, points[-1:]])
    weights = (padded[2:] - padded[:-2]) / 2.0
    factor = np.where((indices == 0) | (indices == resolution - 1), 2.0, 1.0)
    spacing = points[:, None] - points[None, :] + np.eye(resolution)
    parity = np.where((indices[:, None] + indices[None, :]) % 2 == 0, 1.0, -1.0)
    offdiag = (1.0 - np.eye(resolution)) * factor[:, None] / factor[None, :] * parity / spacing
    derivative = offdiag - np.eye(resolution) * offdiag.sum(axis=1)[:, None]
    stiffness = (weights[:, None] * derivative * derivative).sum(axis=0)
    return (points, weights, derivative, stiffness)


def interpolation(fine_count, coarse_count):
    fine_points = tables(fine_count)[0]
    coarse_points = tables(coarse_count)[0]
    columns = []
    for column in range(coarse_count):
        values = np.ones(fine_count)
        for partner in range(coarse_count):
            if partner != column:
                values = (
                    values
                    * (fine_points - coarse_points[partner])
                    / (coarse_points[column] - coarse_points[partner])
                )
        columns.append(values)
    return np.stack(columns, axis=1)


class Columns:
    def __init__(self):
        self.rows, self.index = [], {}

    def add(self, column):
        column = np.asarray(column, np.float32)
        key = tuple(column.tolist())
        if key not in self.index:
            self.index[key] = len(self.rows)
            self.rows.append(column)
        return self.index[key]

    def matrix(self, values):
        full = np.zeros((SUB, SUB))
        full[: values.shape[0], : values.shape[1]] = values
        terms = []
        for shift in range(SUB):
            column = [full[s, (s - shift) % SUB] for s in range(SUB)]
            if np.any(column):
                terms.append((shift, self.add(column)))
        return terms

    def table(self):
        return np.repeat(np.stack(self.rows)[:, :, None], LANES, axis=2)


def padded(values):
    return np.concatenate([values, np.zeros(SUB - len(values))])


def make_plan():
    cols = Columns()
    plan = {}
    for n in (NODES, MID_NODES):
        _, w, d, g = tables(n)
        hat = (d.T @ np.diag(w) @ d) / w[:, None]
        plan[n] = dict(
            n=n, w=w, g=g, hat=hat, along=cols.matrix(hat), wk=cols.add(padded(w)), gk=cols.add(padded(g)),
        )
    pad = np.ones(SUB)
    pad[:MID_NODES] = 0.0
    plan["pad_mid"] = cols.add(pad)
    first, last = np.zeros(SUB), np.zeros(SUB)
    first[0], last[SUB - 1] = 1.0, 1.0
    plan["first"], plan["last"] = cols.add(first), cols.add(last)
    jf = interpolation(NODES, MID_NODES)
    jc = interpolation(MID_NODES, COARSE_NODES)
    plan["jf"], plan["jc"] = jf, jc
    plan["jf_up"], plan["jf_down"] = cols.matrix(jf), cols.matrix(jf.T)
    low = np.zeros(SUB)
    low[:MID_NODES] = 1.0
    plan["low"] = cols.add(low)
    down, up = [], []
    for c in range(3):
        m = np.zeros((SUB, SUB))
        m[2 * c : 2 * c + 2, :MID_NODES] = jc.T
        down.append(cols.matrix(m))
        m = np.zeros((SUB, SUB))
        m[:MID_NODES, 2 * c : 2 * c + 2] = jc
        up.append(cols.matrix(m))
    plan["jc_down"], plan["jc_up"] = down, up
    m = np.zeros((SUB, SUB))
    swap = np.zeros((SUB, SUB))
    for c in range(3):
        for k in range(2):
            swap[2 * c + k, 2 * c + 1 - k] = 1.0
            for e in range(3):
                m[2 * c + k, 2 * e + k] = 1.0
    eye = np.diag(np.where(np.arange(SUB) < 6, 1.0, 0.0))
    plan["derived"] = [cols.matrix(x) for x in (eye - swap, m, m - swap @ m)]
    return plan, cols.table()


PLAN, TABLE = make_plan()


def lane_up(x):
    return pltpu.roll(x, 1, x.ndim - 1)


def lane_down(x):
    return pltpu.roll(x, LANES - 1, x.ndim - 1)


def weigh(scalars, arrays):
    total = None
    for s, x in zip(scalars, arrays):
        s = float(s)
        if s == 0.0:
            continue
        term = x if s == 1.0 else x * s
        total = term if total is None else total + term
    return total


def sublanes(x, terms, tab):
    total = None
    for shift, column in terms:
        moved = x if shift == 0 else pltpu.roll(x, shift, x.ndim - 2)
        term = moved * tab[column]
        total = term if total is None else total + term
    return total


def tree(terms):
    while len(terms) > 1:
        pairs = [terms[i] + terms[i + 1] for i in range(0, len(terms) - 1, 2)]
        terms = pairs + terms[2 * len(pairs) :]
    return terms[0]


def split(matrix, a):
    n = matrix.shape[0]
    half = n // 2
    even = [(matrix[a, j] + matrix[a, n - 1 - j]) / 2 for j in range(half)]
    odd = [(matrix[a, j] - matrix[a, n - 1 - j]) / 2 for j in range(half)]
    return even, odd


def centro(matrix, xs):
    n = matrix.shape[0]
    half = n // 2
    es = [xs[j] + xs[n - 1 - j] for j in range(half)]
    os = [xs[j] - xs[n - 1 - j] for j in range(half)]
    out = [None] * n
    for a in range(half):
        even, odd = split(matrix, a)
        p, q = weigh(even, es), weigh(odd, os)
        out[a], out[n - 1 - a] = p + q, p - q
    return out


def kernel(
    load_hbm, stiff_hbm, bulk_hbm, shift_hbm, contact_hbm, tie_hbm, tab_hbm,
    sol, res,
    load, contact, tab, stiff, bulk, shift, tie, in_sem,
    X, V, EO, B0, FD, FM, RB, G,
    X1, B1, ID1,
    CO, PM, PG, HB, BP, R, D, T, INV, CE,
    load_next, contact_next,
    f_up, f_dn, f_from_prev, f_from_next,
    m_up, m_dn, m_from_prev, m_from_next,
    send, recv,
):
    p8, p4 = PLAN[NODES], PLAN[MID_NODES]
    w8, w4 = p8["w"], p4["w"]
    g = lax.axis_index("group")
    m = lax.axis_index("member")
    loops, members = lax.axis_size("group"), lax.axis_size("member")
    nxt, prv = lax.rem(m + 1, members), lax.rem(m + members - 1, members)
    slot = [0]
    pending = []

    def to_member(src, dst, target):
        i = slot[0]
        slot[0] += 1
        copy = pltpu.make_async_remote_copy(
            src_ref=src, dst_ref=dst, send_sem=send.at[i], recv_sem=recv.at[i],
            device_id={"member": target}, device_id_type=MESH,
        )
        copy.start()
        pending.append(copy)
        return copy

    def to_group(src, dst, offset):
        i = slot[0]
        slot[0] += 1
        copy = pltpu.make_async_remote_copy(
            src_ref=src, dst_ref=dst, send_sem=send.at[i], recv_sem=recv.at[i],
            device_id={"group": lax.rem(g + offset, loops)}, device_id_type=MESH,
        )
        copy.start()
        pending.append(copy)
        return copy

    def near(offset):
        return lax.rem(m + offset + members, members)

    reach = [o for d in range(1, REACH + 1) for o in (d, -d)]
    barrier = pltpu.get_barrier_semaphore()
    for offset in reach:
        pl.semaphore_signal(
            barrier, inc=1, device_id={"member": near(offset)}, device_id_type=MESH
        )
    for offset in range(1, loops):
        pl.semaphore_signal(
            barrier, inc=1, device_id={"group": lax.rem(g + offset, loops)}, device_id_type=MESH
        )
    inputs = [
        pltpu.make_async_copy(src, dst, in_sem.at[i])
        for i, (src, dst) in enumerate(
            (
                (stiff_hbm, stiff), (bulk_hbm, bulk), (shift_hbm, shift), (tie_hbm, tie),
                (tab_hbm, tab), (contact_hbm, contact), (load_hbm, load),
            )
        )
    ]
    for copy in inputs:
        copy.start()
    for copy in inputs[:4]:
        copy.wait()
    pack = PM.at[REACH]
    pack[...] = jnp.concatenate(
        [stiff[...], bulk[...], shift[...], tie[...], jnp.zeros((2, LANES), jnp.float32)], axis=0
    )
    pl.semaphore_wait(barrier, len(reach) + loops - 1)

    setup = [
        to_member(PM.at[REACH], PM.at[REACH - 1], nxt),
        to_member(PM.at[REACH], PM.at[REACH + 1], prv),
        to_member(contact_hbm.at[0], contact_next, prv),
        to_member(load_hbm.at[:, 0], load_next, prv),
    ]
    packs = [
        to_member(PM.at[REACH], PM.at[REACH - o], near(o)) for o in reach if abs(o) > 1
    ]
    pack_prev, pack_next = PM.at[REACH - 1], PM.at[REACH + 1]
    for copy in inputs[4:6]:
        copy.wait()

    def row(ref, i):
        return jnp.broadcast_to(ref[i : i + 1, :], (SUB, LANES))

    def quantities(ref):
        scale = 1.0 + row(ref, 3) * (1.0 / 3.0)
        return [scale * row(ref, 0), scale * row(ref, 1), scale * row(ref, 2), row(ref, 4)]

    third = row(pack, 3) * (1.0 / 3.0)
    CO[0] = third
    for base, plan in ((1, p8), (5, p4)):
        wk = tab[plan["wk"]]
        CO[base] = row(pack, 4) * wk
        for d in range(3):
            CO[base + 1 + d] = row(pack, d) * wk

    own_q = quantities(pack)

    def diagonal(plan, q, a, b):
        w, gg = plan["w"], plan["g"]
        wk, gk = tab[plan["wk"]], tab[plan["gk"]]
        inner = q[0] * float(gg[a] * w[b]) + q[1] * float(w[a] * gg[b]) + q[3] * float(w[a] * w[b])
        return inner * wk + q[2] * gk * float(w[a] * w[b])

    def edge(q):
        return [x + lane_up(x) for x in q]

    def fine_masks(a, ref, q):
        qe = edge(q)
        for b in range(NODES - 1):
            low = jnp.broadcast_to(ref[b, 0:1, :].astype(jnp.float32), (SUB, LANES))
            high = jnp.broadcast_to(ref[b, 1:2, :].astype(jnp.float32), (SUB, LANES))
            free = 1.0 - low * tab[PLAN["first"]] - high * tab[PLAN["last"]]
            FM[a, b] = free
            FD[a, b] = OMEGA * free / diagonal(p8, qe if b == 0 else q, a, b)

    def start_x(c, a, values):
        rhs = FM[a] * values
        B0[c, a] = rhs
        x = FD[a] * rhs
        X[c, a, 0 : NODES - 1] = x
        X[c, a, NODES - 1] = lane_down(x[0])

    for a in range(1, NODES - 1):
        fine_masks(a, contact.at[a], own_q)

    inputs[6].wait()

    @pl.loop(0, 3)
    def _(c):
        for a in range(1, NODES - 1):
            start_x(c, a, load[c, a])

    for copy in setup[:3]:
        copy.wait_recv()
    prev_q = [x + y for x, y in zip(own_q, quantities(pack_prev))]
    next_q = [x + y for x, y in zip(own_q, quantities(pack_next))]
    fine_masks(0, contact.at[0], prev_q)
    fine_masks(NODES - 1, contact_next, next_q)
    setup[3].wait_recv()

    @pl.loop(0, 3)
    def _(c):
        start_x(c, 0, load[c, 0])
        start_x(c, NODES - 1, load_next[c])

    last8 = NODES - 1

    inner = range(1, NODES // 2)

    def fine_prepare(pairs):
        for j in pairs:
            k = last8 - j
            tj = CO[0] * (X[0, j] + X[1, j] + X[2, j])
            tk = CO[0] * (X[0, k] + X[1, k] + X[2, k])
            for c in range(3):
                vj, vk = X[c, j] + tj, X[c, k] + tk
                V[c, j], V[c, k] = vj, vk
                EO[c, j], EO[c, NODES // 2 + j] = vj + vk, vj - vk

    def fine_pair(c, a, planes=None):
        even, odd = split(p8["hat"], a)
        p = weigh(even, [EO[c, j] for j in range(NODES // 2)])
        q = weigh(odd, [EO[c, NODES // 2 + j] for j in range(NODES // 2)])
        out = []
        for plane, ya in ((a, p + q), (last8 - a, p - q)):
            v = V[c, plane]
            yk = sublanes(v, p8["along"], tab)
            base = CO[1] * X[c, plane] + CO[2] * ya + CO[4] * yk
            yb = centro(p8["hat"], [v[b] for b in range(NODES)])
            rows = [
                (base[b] + CO[3] * yb[b]) * float(w8[plane] * w8[b]) for b in range(NODES)
            ]
            rows[0] = rows[0] + lane_up(rows[last8])
            out.append(jnp.stack(rows[:last8], axis=0))
        return out

    def fine_update(c, a, z):
        x = X[c, a, 0:last8] + FD[a] * (B0[c, a] - z)
        X[c, a, 0:last8] = x
        X[c, a, last8] = lane_down(x[0])

    def fine_faces(i, both=True):
        copies = []
        for c in range(3):
            z = fine_pair(c, 0)
            f_dn[i, c], f_up[i, c] = z[0], z[1]
            copies.append([to_member(f_up.at[i, c], f_from_prev.at[i, c], nxt)])
            if both:
                copies[c].append(to_member(f_dn.at[i, c], f_from_next.at[i, c], prv))
        return copies

    def fine_sweep(i, meanwhile=None):
        fine_prepare([0])
        copies = fine_faces(i)

        @pl.loop(0, 3)
        def _(c):
            for a in inner:
                z = fine_pair(c, a)
                fine_update(c, a, z[0])
                fine_update(c, last8 - a, z[1])

        fine_prepare(inner)
        if meanwhile is not None:
            meanwhile()
        for c in range(3):
            for copy in copies[c]:
                copy.wait_recv()
            fine_update(c, 0, f_dn[i, c] + f_from_prev[i, c])
            fine_update(c, last8, f_up[i, c] + f_from_next[i, c])

    last4 = MID_NODES - 1
    coarse_data = {}

    def mid_setup():
        for copy in packs:
            copy.wait_recv()
        coarse_data["packs"] = [to_group(PM, PG.at[g], o) for o in range(1, loops)]
        pad = tab[PLAN["pad_mid"]]
        for a in range(MID_NODES):
            q = prev_q if a == 0 else next_q if a == last4 else own_q
            qe = edge(q)
            for b in range(last4):
                ID1[a, b] = OMEGA / (diagonal(p4, qe if b == 0 else q, a, b) + pad)

    low = tab[PLAN["low"]]

    def bundle(z):
        tiles = [z[c, b] for c in range(3) for b in range(last4)]
        rows = [tiles[2 * i] + pltpu.roll(tiles[2 * i + 1], 4, 0) for i in range(4)]
        return jnp.stack(rows + [tiles[8]], axis=0)

    def unbundle(rows):
        tiles = []
        for i in range(4):
            tiles.append(rows[i] * low)
            tiles.append(pltpu.roll(rows[i], 4, 0) * low)
        tiles.append(rows[4])
        return jnp.stack([jnp.stack(tiles[3 * c : 3 * c + 3], axis=0) for c in range(3)], axis=0)

    def mid_apply():
        us = [X1[a] for a in range(MID_NODES)]
        vs = [u + CO[0] * jnp.sum(u, axis=0, keepdims=True) for u in us]
        half = MID_NODES // 2
        es = [vs[j] + vs[last4 - j] for j in range(half)]
        os = [vs[j] - vs[last4 - j] for j in range(half)]

        def pair(a):
            even, odd = split(p4["hat"], a)
            p, q = weigh(even, es), weigh(odd, os)
            out = []
            for plane, ya in ((a, p + q), (last4 - a, p - q)):
                yk = sublanes(vs[plane], p4["along"], tab)
                base = CO[5] * us[plane] + CO[6] * ya + CO[8] * yk
                yb = centro(p4["hat"], [vs[plane][:, b] for b in range(MID_NODES)])
                rows = [
                    (base[:, b] + CO[7] * yb[b]) * float(w4[plane] * w4[b])
                    for b in range(MID_NODES)
                ]
                rows[0] = rows[0] + lane_up(rows[last4])
                out.append(jnp.stack(rows[:last4], axis=1))
            return out

        return pair

    def mid_store(a, x):
        X1[a, :, 0:last4] = x
        X1[a, :, last4] = lane_down(x[:, 0])

    mid_slot = [0]

    def mid_exchange(low_face, high_face):
        i = mid_slot[0]
        mid_slot[0] += 1
        m_dn[i], m_up[i] = bundle(low_face), bundle(high_face)
        up = to_member(m_up.at[i], m_from_prev.at[i], nxt)
        down = to_member(m_dn.at[i], m_from_next.at[i], prv)

        def arrive():
            up.wait_recv()
            down.wait_recv()
            return unbundle(m_from_prev[i]), unbundle(m_from_next[i])

        return arrive

    def mid_sweep():
        pair = mid_apply()
        faces = pair(0)
        arrive = mid_exchange(faces[0], faces[1])
        z = [faces[0], *pair(1), faces[1]]

        def update(a, total):
            mid_store(a, X1[a, :, 0:last4] + ID1[a] * (B1[a] - total))

        for a in range(1, last4):
            update(a, z[a])
        below, above = arrive()
        update(0, z[0] + below)
        update(last4, z[last4] + above)

    def wide_row(x):
        return jnp.broadcast_to(x, (SUB, LANES))

    def coarse_setup():
        for copy in coarse_data["packs"]:
            copy.wait_recv()
        PG[g] = PM[...]
        for i in range(PLANES):
            T[0, i] = jnp.zeros((SUB, LANES), jnp.float32)
        for s in range(2):
            for i in range(PLANES):
                D[s, 0, i] = jnp.zeros((SUB, LANES), jnp.float32)
                D[s, loops + 1, i] = jnp.zeros((SUB, LANES), jnp.float32)

        @pl.loop(0, loops)
        def _(h):
            alive = jnp.where(h < loops - 1, jnp.float32(1.0), jnp.float32(0.0))
            for i in range(PLANES):
                T[h + 1, i] = wide_row(PG[h, i + 1, 5:6, :] * alive)

        @pl.loop(0, loops)
        def _(h):
            parts = []
            for j in range(SPAN):
                s0, s1, s2 = (PG[h, j, d : d + 1, :] for d in range(3))
                b, t = PG[h, j, 3:4, :], PG[h, j, 4:5, :]
                parts.append((1.0 + b * (1.0 / 3.0)) * (s0 + s1 + s2) * 0.5 + t)
                if 1 <= j < SPAN - 1:
                    for k, x in enumerate((s0 * 0.5, s1 * 0.5, s2 * 0.5, t, b * (1.0 / 3.0))):
                        CE[k, h, j - 1] = wide_row(x)
            for i in range(PLANES):
                e = wide_row(parts[i] + parts[i + 1])
                INV[h, i] = 1.0 / (e + lane_up(e) + T[h + 1, i] + T[h, i])

    def coarse_step(s, h, first, second):
        now, later = s % 2, 1 - s % 2
        low, high = s, PLANES - 1 - s

        def derived(i):
            u = D[now, h + 1, i]
            rolled = [u] + [pltpu.roll(u, r, 0) for r in range(1, SUB)]
            four = [u]
            for terms in PLAN["derived"]:
                four.append(tree([rolled[r] * tab[column] for r, column in terms]))
            return four, [lane_down(x) for x in four]

        carry = None
        left = derived(low)
        for e in range(low, high):
            right = derived(e + 1)
            h0, h1, h2, react, th = (CE[k, h, e] for k in range(5))
            v = [[x[0] + th * x[2] for x in side] for side in (left, right)]
            w = [[x[1] + th * x[3] for x in side] for side in (left, right)]
            u = [[x[0] for x in side] for side in (left, right)]
            da = [h0 * (v[0][b] - v[1][b]) for b in range(2)]
            db = [h1 * (v[a][0] - v[a][1]) for a in range(2)]
            sums = []
            for a in range(2):
                rows = []
                for b in range(2):
                    x = react * u[a][b] + h2 * w[a][b]
                    x = x + da[b] if a == 0 else x - da[b]
                    rows.append(x + db[a] if b == 0 else x - db[a])
                sums.append(rows[0] + lane_up(rows[1]))
            if carry is not None:
                d = D[now, h + 1, e]
                t, tu = T[h + 1, e], T[h, e]
                z = sums[0] + carry
                z = z + t * (d - D[now, h + 2, e]) + tu * (d - D[now, h, e])
                r = R[h, e] - z
                R[h, e] = r
                D[later, h + 1, e] = first * d + second * INV[h, e] * r
            carry = sums[1]
            left = right

    fine_prepare(inner)
    fine_sweep(0, mid_setup)

    jf, jc = PLAN["jf"], PLAN["jc"]
    fine_prepare([0])

    @pl.loop(0, 3)
    def _(c):
        for a in range(NODES // 2):
            z = fine_pair(c, a)
            for plane, value in ((a, z[0]), (last8 - a, z[1])):
                r = FM[plane] * value
                r = -r if plane == last8 else B0[c, plane] - r
                for bc in range(MID_NODES):
                    RB[plane, bc] = weigh(jf[:last8, bc], [r[b] for b in range(last8)])
        for plane in range(NODES):
            RB[plane, 0] = RB[plane, 0] + lane_up(RB[plane, last4])
        for ac in range(MID_NODES):
            part = weigh(jf[:, ac], [RB[a, 0:last4] for a in range(NODES)])
            G[ac, c] = sublanes(part, PLAN["jf_down"], tab)

    arrive = mid_exchange(G[0], G[last4])
    for a in range(1, last4):
        B1[a] = G[a]
        mid_store(a, ID1[a] * G[a])
    coarse_setup()
    below, above = arrive()
    for a, extra in ((0, below), (last4, above)):
        b1 = G[a] + extra
        B1[a] = b1
        mid_store(a, ID1[a] * b1)

    mid_sweep()
    pair = mid_apply()
    faces = pair(0)
    z = [faces[0], *pair(1), faces[1]]
    rs = [B1[a] - z[a] for a in range(last4)] + [-z[last4]]
    hs = []
    for ac in range(2):
        part = weigh(jc[:, ac], rs)
        along = [weigh(jc[:last4, bc], [part[:, b] for b in range(last4)]) for bc in range(2)]
        along = along[0] + lane_up(along[1])
        total = None
        for c in range(3):
            term = sublanes(along[c], PLAN["jc_down"][c], tab)
            total = term if total is None else total + term
        hs.append(total)
    HB[REACH, 0], HB[REACH, 1] = hs[0], hs[1]
    halo = [to_member(HB.at[REACH], HB.at[REACH - o], near(o)) for o in reach]
    inside = REACH - 2
    for copy in halo[: 2 * inside]:
        copy.wait_recv()
    mid_low, mid_high = inside, PLANES - inside
    others = []

    def planes_out(low, high):
        for o in range(1, loops):
            cut = min(o, loops - o)
            first, last = max(low, cut), min(high, PLANES - cut)
            if first < last:
                part = pl.ds(first, last - first)
                others.append(to_group(BP.at[part], R.at[g, part], o))

    for i in range(mid_low, mid_high):
        BP[i] = HB[i + 1, 0] + HB[i, 1]
    planes_out(mid_low, mid_high)
    for copy in halo[2 * inside :]:
        copy.wait_recv()
    for i in [*range(mid_low), *range(mid_high, PLANES)]:
        BP[i] = HB[i + 1, 0] + HB[i, 1]
    planes_out(0, mid_low)
    planes_out(mid_high, PLANES)
    R[g] = BP[...]
    center = 0.5 * (UPPER_BOUND + LOWER_BOUND)
    radius = 0.5 * (UPPER_BOUND - LOWER_BOUND)
    ratio = center / radius
    damping_now = 1.0 / ratio
    for copy in others:
        copy.wait_recv()

    @pl.loop(0, loops)
    def _(h):
        for i in range(PLANES):
            D[0, h + 1, i] = INV[h, i] * R[h, i] * (1.0 / center)

    x2 = [D[0, g + 1, REACH - 1], D[0, g + 1, REACH]]
    for s in range(CHEB - 1):
        damping_next = 1.0 / (2.0 * ratio - damping_now)
        first, second = damping_next * damping_now, 2.0 * damping_next / radius
        if s < CHEB - 2:
            for h in range(loops):
                coarse_step(s, h, first, second)
        else:
            coarse_step(s, g, first, second)
        damping_now = damping_next
        x2 = [x + D[1 - s % 2, g + 1, REACH - 1 + a] for a, x in enumerate(x2)]

    wide = [[x, lane_down(x)] for x in x2]
    lifted = []
    for a in range(2):
        lifted.append(
            [
                jnp.stack([sublanes(wide[a][b], PLAN["jc_up"][c], tab) for c in range(3)], axis=0)
                for b in range(2)
            ]
        )
    for a in range(MID_NODES):
        cross = [weigh(jc[a], [lifted[0][b], lifted[1][b]]) for b in range(2)]
        add = jnp.stack([weigh(jc[b], cross) for b in range(last4)], axis=1)
        mid_store(a, X1[a, :, 0:last4] + add)
    mid_sweep()
    mid_sweep()

    @pl.loop(0, 3)
    def _(c):
        for a in range(MID_NODES):
            RB[a] = sublanes(X1[a, c], PLAN["jf_up"], tab)
        for a in range(NODES):
            part = weigh(jf[a], [RB[i] for i in range(MID_NODES)])
            add = jnp.stack(
                [weigh(jf[b], [part[i] for i in range(MID_NODES)]) for b in range(last8)], axis=0
            )
            x = X[c, a, 0:last8] + FM[a] * add
            X[c, a, 0:last8] = x
            X[c, a, last8] = lane_down(x[0])

    fine_prepare(inner)
    fine_sweep(1)
    fine_sweep(2)

    fine_prepare([0])
    final = fine_faces(3, both=False)

    @pl.loop(0, 3)
    def _(c):
        for a in range(1, NODES // 2):
            z = fine_pair(c, a)
            res[c, a] = B0[c, a] - FM[a] * z[0]
            res[c, last8 - a] = B0[c, last8 - a] - FM[last8 - a] * z[1]
        for a in range(last8):
            sol[c, a] = X[c, a, 0:last8]

    for c in range(3):
        final[c][0].wait_recv()
        res[c, 0] = B0[c, 0] - FM[0] * (f_dn[3, c] + f_from_prev[3, c])

    for copy in pending:
        copy.wait_send()


def write_out(sol, res, sol_hbm, res_hbm, sem):
    copies = [
        pltpu.make_async_copy(src.at[c], dst.at[c], sem.at[2 * c + i])
        for c in range(3)
        for i, (src, dst) in enumerate(((sol, sol_hbm), (res, res_hbm)))
    ]
    for copy in copies:
        copy.start()
    for copy in copies:
        copy.wait()


def body(load, stiffness_dir, bulk_ratio, thermal_shift, contact, loop_tie):
    f32 = jnp.float32
    n, q, o = NODES, MID_NODES, NODES - 1
    tile = (SUB, LANES)

    def vmem(*shape):
        return pltpu.VMEM(shape, f32)

    spec = pl.BlockSpec(memory_space=pltpu.VMEM)
    slots = 80
    loops = lax.axis_size("group")
    hbm = pl.BlockSpec(memory_space=pltpu.HBM)
    scratch = [
        vmem(3, o, o, *tile), pltpu.VMEM((o, o, 2, LANES), jnp.int32), vmem(*TABLE.shape),
        vmem(3, LANES), vmem(1, LANES), vmem(1, LANES), vmem(1, LANES),
        pltpu.SemaphoreType.DMA((7,)),
        vmem(3, n, n, *tile), vmem(3, n, n, *tile), vmem(3, n, n, *tile),
        vmem(3, n, o, *tile), vmem(n, o, *tile), vmem(n, o, *tile),
        vmem(n, q, *tile), vmem(q, 3, q - 1, *tile),
        vmem(q, 3, q, *tile), vmem(q, 3, q - 1, *tile), vmem(q, q - 1, *tile),
        vmem(9, *tile),
        vmem(SPAN, *tile), vmem(loops, SPAN, *tile), vmem(SPAN, 2, *tile),
        vmem(PLANES, *tile), vmem(loops, PLANES, *tile),
        vmem(2, loops + 2, PLANES, *tile), vmem(loops + 1, PLANES, *tile),
        vmem(loops, PLANES, *tile), vmem(5, loops, PLANES - 1, *tile),
        vmem(3, o, *tile), pltpu.VMEM((o, 2, LANES), jnp.int32),
    ]
    scratch += [vmem(4, 3, o, *tile) for _ in range(4)]
    scratch += [vmem(4, 5, *tile) for _ in range(4)]
    scratch += [
        pltpu.SemaphoreType.DMA((slots,)),
        pltpu.SemaphoreType.DMA((slots,)),
    ]
    shape = jax.ShapeDtypeStruct(load.shape, f32)
    outputs = pl.pallas_call(
        kernel,
        out_shape=(shape, shape),
        in_specs=[hbm] * 7,
        out_specs=(spec, spec),
        scratch_shapes=scratch,
        compiler_params=pltpu.CompilerParams(
            collective_id=0, has_side_effects=True, vmem_limit_bytes=48 * 2**20
        ),
    )(
        *(
            pltpu.with_memory_space_constraint(x, pltpu.HBM)
            for x in (
                load,
                stiffness_dir,
                bulk_ratio.reshape(1, LANES),
                thermal_shift.reshape(1, LANES),
                contact.transpose(1, 2, 0, 3),
                loop_tie.reshape(1, LANES),
                jnp.asarray(TABLE),
            )
        )
    )
    return pl.pallas_call(
        write_out,
        out_shape=(shape, shape),
        in_specs=[spec, spec],
        out_specs=(hbm, hbm),
        scratch_shapes=[pltpu.SemaphoreType.DMA((6,))],
        compiler_params=pltpu.CompilerParams(vmem_limit_bytes=2**20),
    )(*outputs)


def solution(mesh):
    in_specs = (
        P(None, None, None, None, ("group", "member")),
        P(None, ("group", "member")),
        P(("group", "member")),
        P(("group", "member")),
        P(None, None, None, ("group", "member")),
        P(("group", "member")),
    )
    out_specs = (
        P(None, None, None, None, ("group", "member")),
        P(None, None, None, None, ("group", "member")),
    )
    return jax.shard_map(body, mesh=mesh, in_specs=in_specs, out_specs=out_specs, check_vma=False)
```
